256 devices in a mesh: space: 32 (over y, x, z_hi), band: 8 (over z_lo, core).
Axes of the slice: x: 4, y: 4, z: 8 (z_hi: 2, z_lo: 4; z = z_hi * 4 + z_lo), core: 2. Of those that a mesh axis runs over, the one named last changes fastest.
Arguments:
- orbitals: float32 [64, 192, 32, 128], P('band', 'space'), may hold values from -18 to 18
- previous: float32 [64, 192, 32, 128], P('band', 'space'), may hold values from -18 to 18
- potential: float32 [192, 32, 128], P('space'), may hold values from -4 to 4
- projectors: bfloat16 [128, 9, 6, 32, 128], P('space'), may hold values from -0.1875 to 0.1875
- strengths: float32 [128, 9], replicated, may hold values from -3 to 3
- atom_planes: int32 [128], replicated, may hold values from 0 to 191, as said below
Outputs:
- filtered: bfloat16 [64, 192, 32, 128], P('band', 'space')
- margin: float32 [64, 64], P('space', 'band')
- projection: float32 [64, 64], P('space', 'band')
The draws below stay inside these ranges and needn't reach their ends.
Inputs may be any that keep to these rules, and one draw needn't show every extreme that they name: `atom_planes`: entry a is the first plane of atom a's box of 6 planes. In each aligned block of 4 entries (block s) every box starts at one of the planes s * 6 to s * 6 + 5, and in every block one atom starts at the first of these planes and another at the last.
All inputs are finite; a program needn't handle non-finite values.
Results may differ from the reference program's by a relative error of at most 0.0065.
Values may be sent and summed in bfloat16 or wider, within the bound.
A program may use at most 192 MiB of HBM per device.

```python
import math
import jax
import jax.numpy as jnp
from jax import lax

CX = 6
NY = 32
NZ = 128
ATOM_DEV = 4
HALO = 6
BOX = 6
NPJ = 9
NX = 192
BANDS = 64
ATOMS = 128


def draw_atom_planes(key, part):
    slab_count = ATOMS // ATOM_DEV
    key_offsets = jax.random.fold_in(key, 11)
    key_first = jax.random.fold_in(key, 12)
    key_stride = jax.random.fold_in(key, 13)
    offsets = jax.random.randint(key_offsets, (slab_count, ATOM_DEV), 0, CX, dtype=jnp.int32)
    first = jax.random.randint(key_first, (slab_count, 1), 0, ATOM_DEV, dtype=jnp.int32)
    stride = jax.random.randint(key_stride, (slab_count, 1), 1, ATOM_DEV, dtype=jnp.int32)
    second = (first + stride) % ATOM_DEV
    column = jnp.arange(ATOM_DEV, dtype=jnp.int32)[None, :]
    offsets = jnp.where(column == first, 0, jnp.where(column == second, CX - 1, offsets))
    anchor = jnp.arange(slab_count, dtype=jnp.int32)[:, None] * CX
    return (anchor + offsets).reshape(-1).astype(jnp.int32)


def rough_values(key, shape):
    return jnp.clip(jax.random.normal(key, shape, jnp.float32), -3.0, 3.0)


def plane_envelope():
    planes = jnp.arange(NX, dtype=jnp.float32) / NX
    return 0.5 * jnp.exp(jnp.log(3.0) * planes)


def mixed_bands(key, salt, factor_low, factor_high):
    noise = rough_values(jax.random.fold_in(key, salt), (BANDS, NX, NY, NZ))
    shifts = jax.random.randint(jax.random.fold_in(key, salt + 1), (3,), 1, BANDS, dtype=jnp.int32)
    mixing = jax.random.uniform(jax.random.fold_in(key, salt + 2), (3,), jnp.float32, 0.2, 0.3)
    total = noise
    for index in range(3):
        total = total + mixing[index] * jnp.roll(noise, shifts[index], axis=0)
    factors = jax.random.uniform(jax.random.fold_in(key, salt + 3), (BANDS,), jnp.float32, factor_low, factor_high)
    envelope = plane_envelope()
    return factors[:, None, None, None] * envelope[None, :, None, None] * total


def draw_orbitals(key, part):
    return mixed_bands(key, 51, 0.6, 1.4)


def draw_previous(key, part):
    return mixed_bands(key, 61, 0.3, 0.8)


def shard_levels(rng, dims, shards, smallest, top_value):
    gain, own = 1.0, jax.random.fold_in(rng, 6)
    for dim, blocks in shards:
        heights = jnp.exp(jax.random.uniform(jax.random.fold_in(own, dim), (blocks,), jnp.float32, smallest / len(shards), top_value / len(shards)))
        gain = gain * jnp.repeat(heights, dims[dim] // blocks).reshape([-1 if axis == dim else 1 for axis in range(len(dims))])
    return gain


def centred(rng, extent, scale, most, split=(), kind=jnp.bfloat16):
    result = scale * jax.random.normal(rng, extent, jnp.float32)
    if split:
        result = result * shard_levels(rng, extent, split, -0.22, 0.18)
    return jnp.clip(result, -most, most).astype(kind)


def setup_inputs(seed: int = 0) -> dict:
    keys = jax.random.split(jax.random.key(seed), 7)
    return {
        "orbitals": draw_orbitals(jax.random.fold_in(keys[6], 71), 0),
        "previous": draw_previous(jax.random.fold_in(keys[6], 71), 0),
        "potential": centred(keys[2], (NX, NY, NZ), 1.0, 4.0, ((0, 32),), jnp.float32),
        "projectors": centred(keys[3], (ATOMS, NPJ, BOX, NY, NZ), (0.4 / (BOX * NY * NZ) ** 0.25), 0.1875, ((0, 32),)),
        "strengths": jnp.clip(jax.random.uniform(keys[4], (ATOMS, NPJ), jnp.float32, -3.0, 3.0), -3.0, 3.0),
        "atom_planes": draw_atom_planes(jax.random.fold_in(keys[6], 71), 0),
    }


stencil_weights = (-5369.0 / 1800.0, 12.0 / 7.0, -15.0 / 56.0, 10.0 / 189.0, -1.0 / 112.0, 2.0 / 1925.0, -1.0 / 16632.0)
center = 5.5
halfwidth = 5.5


def laplace_axis(field, axis):
    total = stencil_weights[0] * field
    for offset in range(1, HALO + 1):
        total = total + stencil_weights[offset] * (jnp.roll(field, offset, axis) + jnp.roll(field, -offset, axis))
    return total


def reference(orbitals, previous, potential, projectors, strengths, atom_planes):
    block = math.gcd(BANDS, 32)
    count = BANDS // block
    projector_values = projectors.astype(jnp.float32)

    def filter_block(block_pair):
        psi_block, prev_block = block_pair
        kinetic = -0.5 * (laplace_axis(psi_block, 1) + laplace_axis(psi_block, 2) + laplace_axis(psi_block, 3))

        def per_atom(accumulated, inputs):
            first_plane, values, scales = inputs
            planes = ((first_plane + jnp.arange(BOX, dtype=jnp.int32)) % NX).astype(jnp.int32)
            box_values = jnp.take(psi_block, planes, axis=1)
            coefficients = jnp.einsum("jpyz,bpyz->jb", values, box_values, precision=lax.Precision.HIGHEST)
            added = jnp.einsum("jpyz,jb->bpyz", values, coefficients * scales[:, None], precision=lax.Precision.HIGHEST)
            return accumulated.at[:, planes].add(added), None

        projected, unused = lax.scan(per_atom, jnp.zeros_like(psi_block), (atom_planes, projector_values, strengths))
        hamil = kinetic + potential[None] * psi_block + projected
        return ((2.0 / halfwidth) * (hamil - center * psi_block) - prev_block).astype(jnp.bfloat16)

    filtered = lax.map(filter_block, (orbitals.reshape(count, block, NX, NY, NZ), previous.reshape(count, block, NX, NY, NZ)))
    filtered = filtered.reshape(BANDS, NX, NY, NZ)
    scale = 1.0 / (NX * NY * NZ)
    rows = filtered.reshape(BANDS, -1)
    panel = orbitals.astype(jnp.bfloat16).reshape(BANDS, -1)
    margin = jnp.dot(rows, rows.T, preferred_element_type=jnp.float32) * scale
    projection = jnp.dot(rows, panel.T, preferred_element_type=jnp.float32) * scale
    return filtered, margin, projection
```

```python
import jax
import jax.numpy as jnp
from jax import lax
from jax.experimental import pallas as pl
from jax.experimental.pallas import tpu as pltpu
from jax.sharding import PartitionSpec as P

HALO = 6
BOX = 6
NPJ = 9


stencil_weights = (
    -5369.0 / 1800.0,
    12.0 / 7.0,
    -15.0 / 56.0,
    10.0 / 189.0,
    -1.0 / 112.0,
    2.0 / 1925.0,
    -1.0 / 16632.0,
)
center = 5.5
halfwidth = 5.5


def with_halo(block, sides, width):
    for axis, dim in sides:
        count = lax.axis_size(axis)
        forward = [(i, i + 1) for i in range(count - 1)]
        forward.append((count - 1, 0))
        backward = [(target, source) for source, target in forward]
        low = lax.ppermute(
            lax.slice_in_dim(block, block.shape[dim] - width, None, axis=dim), axis, forward
        )
        high = lax.ppermute(lax.slice_in_dim(block, 0, width, axis=dim), axis, backward)
        block = jnp.concatenate([low, block, high], axis=dim)
    return block


def shifted(value, axis, steps):
    count = lax.axis_size(axis)
    pairs = [(source, (source + steps) % count) for source in range(count)]
    return lax.ppermute(value, axis, pairs)


def laplace_axis(field, axis):
    total = stencil_weights[0] * field
    for offset in range(1, HALO + 1):
        total = total + stencil_weights[offset] * (
            jnp.roll(field, offset, axis) + jnp.roll(field, -offset, axis)
        )
    return total


def place_table(first_planes, projector_block, base, window, total_planes):
    box_rows = jnp.arange(BOX, dtype=jnp.int32)
    planes_out = jnp.arange(window, dtype=jnp.int32)
    relative = (first_planes[:, None] + box_rows[None, :] - base) % total_planes
    placer = (planes_out[None, None, :] == relative[:, :, None]).astype(jnp.float32)
    return jnp.einsum(
        "apq,ajpyz->ajqyz",
        placer,
        projector_block.astype(jnp.float32),
        precision=lax.Precision.HIGHEST,
    )


def scatter_sum_kernel(parts_ref, out_ref, arrived, send_sem, recv_sem):
    count = parts_ref.shape[0]
    me = lax.axis_index("space")
    barrier = pltpu.get_barrier_semaphore()
    for step in range(1, count):
        peer = lax.rem(me + step, count)
        pl.semaphore_signal(
            barrier, inc=1, device_id={"space": peer}, device_id_type=pl.DeviceIdType.MESH
        )
    arrived[0] = parts_ref[me]
    pl.semaphore_wait(barrier, count - 1)
    copies = []
    for step in range(1, count):
        peer = lax.rem(me + step, count)
        copy = pltpu.make_async_remote_copy(
            src_ref=parts_ref.at[peer],
            dst_ref=arrived.at[step],
            send_sem=send_sem.at[step],
            recv_sem=recv_sem.at[step],
            device_id={"space": peer},
            device_id_type=pl.DeviceIdType.MESH,
        )
        copy.start()
        copies.append(copy)
    for copy in copies:
        copy.wait()
    out_ref[...] = jnp.sum(arrived[...], axis=0)


def scatter_sum(partial_sums):
    count = lax.axis_size("space")
    rows, columns = partial_sums.shape[0] // count, partial_sums.shape[1]
    parts = partial_sums.reshape(count, 1, rows * columns)
    parts = jnp.pad(parts, ((0, 0), (0, 0), (0, 128 - rows * columns)))
    total = pl.pallas_call(
        scatter_sum_kernel,
        out_shape=jax.ShapeDtypeStruct((1, 128), jnp.float32),
        in_specs=[pl.BlockSpec(memory_space=pltpu.VMEM)],
        out_specs=pl.BlockSpec(memory_space=pltpu.VMEM),
        scratch_shapes=[
            pltpu.VMEM((count, 1, 128), jnp.float32),
            pltpu.SemaphoreType.DMA((count,)),
            pltpu.SemaphoreType.DMA((count,)),
        ],
        compiler_params=pltpu.CompilerParams(collective_id=0, has_side_effects=True),
        name="scatter_sum",
    )(parts)
    return total[0, : rows * columns].reshape(rows, columns)


def shards(orbitals, previous, potential, projectors, strengths, atom_planes):
    band_dev, slab_planes, cells_y, cells_z = orbitals.shape
    space_count = lax.axis_size("space")
    total_planes = slab_planes * space_count
    extended = with_halo(orbitals, (("space", 1),), HALO)
    along_x = stencil_weights[0] * orbitals
    for offset in range(1, HALO + 1):
        ahead = extended[:, HALO + offset : HALO + offset + slab_planes]
        behind = extended[:, HALO - offset : HALO - offset + slab_planes]
        along_x = along_x + stencil_weights[offset] * (ahead + behind)
    kinetic = -0.5 * (along_x + laplace_axis(orbitals, 2) + laplace_axis(orbitals, 3))
    device_index = lax.axis_index("space")
    atom_count = projectors.shape[0]
    own_start = device_index * atom_count
    own_planes = lax.dynamic_slice_in_dim(atom_planes, own_start, atom_count, 0)
    own_strengths = lax.dynamic_slice_in_dim(strengths, own_start, atom_count, 0)
    table = place_table(
        own_planes, projectors, device_index * slab_planes, slab_planes + HALO, total_planes
    )
    table_flat = table.reshape(atom_count * NPJ, -1)
    upper = extended[:, HALO:].reshape(band_dev, -1)
    coefficients = lax.dot_general(
        table_flat,
        upper,
        (((1,), (1,)), ((), ())),
        precision=lax.Precision.HIGHEST,
        preferred_element_type=jnp.float32,
    )
    weighted = coefficients * own_strengths.reshape(-1)[:, None]
    added = lax.dot_general(
        weighted,
        table_flat,
        (((0,), (0,)), ((), ())),
        precision=lax.Precision.HIGHEST,
        preferred_element_type=jnp.float32,
    )
    added = added.reshape(band_dev, slab_planes + HALO, cells_y, cells_z)
    arrived = shifted(added[:, slab_planes:].astype(jnp.bfloat16), "space", 1).astype(jnp.float32)
    padding = jnp.zeros((band_dev, slab_planes - HALO, cells_y, cells_z), jnp.float32)
    projected_term = added[:, :slab_planes] + jnp.concatenate([arrived, padding], 1)
    hamil = kinetic + potential[None] * orbitals + projected_term
    filtered = (2.0 / halfwidth * (hamil - center * orbitals) - previous).astype(jnp.bfloat16)
    scale = 1.0 / (slab_planes * space_count * cells_y * cells_z)
    filtered_flat = filtered.reshape(band_dev, -1)
    panel_flat = orbitals.astype(jnp.bfloat16).reshape(band_dev, -1)
    columns_right = jnp.concatenate([filtered_flat, panel_flat], 0)
    piece = lax.all_gather(filtered, "band", axis=0, tiled=True)
    rows = piece.reshape(piece.shape[0], -1)
    products = lax.dot_general(
        rows, columns_right, (((1,), (1,)), ((), ())), preferred_element_type=jnp.float32
    )
    partial_sums = products * scale
    shares = scatter_sum(partial_sums)
    margin = shares[:, :band_dev]
    projection = shares[:, band_dev:]
    return (filtered, margin, projection)


def solution(mesh):
    in_specs = (
        P("band", "space", None, None),
        P("band", "space", None, None),
        P("space", None, None),
        P("space", None, None, None, None),
        P(),
        P(),
    )
    out_specs = (P("band", "space", None, None), P("space", "band"), P("space", "band"))
    return jax.shard_map(shards, mesh=mesh, in_specs=in_specs, out_specs=out_specs, check_vma=False)
```

```python
import jax
import jax.numpy as jnp
from jax import lax
from jax.experimental import pallas as pl
from jax.experimental.pallas import tpu as pltpu
from jax.sharding import PartitionSpec as P

MESH = pl.DeviceIdType.MESH
BF = jnp.bfloat16
F32 = jnp.float32

HALO = 6
BOX = 6
NPJ = 9
ATOM_DEV = 4
RING = 16
GROUP = 8
COLUMNS = 16
SIDE = 4
SLABS = 32
PAD = BOX - 1
ORDER = (1, 15, 2, 14, 3, 13, 4, 12, 5, 11, 6, 10, 7, 9, 8)

stencil_weights = (
    -5369.0 / 1800.0,
    12.0 / 7.0,
    -15.0 / 56.0,
    10.0 / 189.0,
    -1.0 / 112.0,
    2.0 / 1925.0,
    -1.0 / 16632.0,
)
center = 5.5
halfwidth = 5.5
gain = 2.0 / halfwidth


def nt_dot(a, b):
    return lax.dot_general(a, b, (((1,), (1,)), ((), ())), preferred_element_type=F32)


def step_kernel(
    scale,
    planes_ref,
    psi_ref,
    prev_ref,
    pot_ref,
    own_proj_ref,
    far_proj_ref,
    strength_ref,
    filtered_ref,
    gram_ref,
    psi_send,
    local_send,
    window,
    local_got,
    filt_send,
    proj,
    proj_low,
    along_x,
    coef_acc,
    coef_send,
    coef_got,
    coef_mine,
    coef_all,
    gram_acc,
    gram_y_send,
    gram_y_got,
    gram_x_send,
    gram_x_got,
    gram_z_send,
    gram_z_got,
    psi_ss,
    psi_rs,
    halo_ss,
    halo_rs,
    proj_ss,
    proj_rs,
    local_ss,
    local_rs,
    red_ss,
    red_rs,
    all_ss,
    all_rs,
    filt_ss,
    filt_rs,
    gy_ss,
    gy_rs,
    gx_ss,
    gx_rs,
    gz_ss,
    gz_rs,
):
    space = lax.axis_index("space")
    band = lax.axis_index("band")
    column, half = space // 2, lax.rem(space, 2)
    col_y, col_x = column // SIDE, lax.rem(column, SIDE)
    me = half * GROUP + band

    def ring(k):
        return lax.rem(me + k, RING)

    def at_ring(index):
        return {"space": column * 2 + index // GROUP, "band": lax.rem(index, GROUP)}

    def at_column(col):
        return {"space": lax.rem(col + COLUMNS, COLUMNS) * 2 + half, "band": band}

    def remote(src, dst, ssem, rsem, device):
        return pltpu.make_async_remote_copy(
            src_ref=src, dst_ref=dst, send_sem=ssem, recv_sem=rsem,
            device_id=device, device_id_type=MESH,
        )

    mirror = (1 - half) * GROUP + (3 - band // 2) * 2 + lax.rem(band, 2)

    barrier = pltpu.get_barrier_semaphore()
    peers = [at_ring(ring(k)) for k in ORDER]
    peers += [at_column(lax.rem(col_y + k, SIDE) * SIDE + col_x) for k in (1, 2, 3)]
    peers += [at_column(col_y * SIDE + lax.rem(col_x + k, SIDE)) for k in (1, 2, 3)]
    peers += [at_column(column + 1), at_column(column - 1)]
    for peer in peers:
        pl.semaphore_signal(barrier, inc=1, device_id=peer, device_id_type=MESH)

    def pack(p, carry):
        psi_send[:, p] = psi_ref[p].reshape(RING, 16, 128).astype(BF)
        return carry

    lax.fori_loop(0, HALO, pack, 0)
    for k in range(3):
        table = proj.at[k - 1] if k else proj_low
        table[:, 0:PAD] = jnp.zeros((ATOM_DEV, PAD, 32, 128), BF)
        table[:, PAD + BOX :] = jnp.zeros((ATOM_DEV, BOX, 32, 128), BF)
    proj[half, :, PAD : PAD + BOX] = own_proj_ref[...]
    window[1 + half, band] = psi_send[me]

    pl.semaphore_wait(barrier, len(peers))

    inner = pl.ds(PAD, BOX)
    sends = []
    for k in ORDER:
        copy = remote(
            psi_send.at[ring(k)], window.at[1 + half, band], psi_ss.at[k], psi_rs.at[k],
            at_ring(ring(k)),
        )
        copy.start()
        sends.append(copy)
    copy = remote(
        far_proj_ref, proj.at[half, :, inner], proj_ss.at[0], proj_rs.at[0], at_ring(mirror)
    )
    copy.start()
    sends.append(copy)

    def local_terms(p, carry):
        field = psi_ref[p]
        flat = field.reshape(256, 128)
        total = (3.0 * stencil_weights[0]) * field
        for m in range(1, HALO + 1):
            ahead = jnp.concatenate([field[m:], field[:m]], axis=0)
            behind = jnp.concatenate([field[32 - m :], field[: 32 - m]], axis=0)
            turned = pltpu.roll(flat, m, 1) + pltpu.roll(flat, 128 - m, 1)
            total = total + stencil_weights[m] * (ahead + behind + turned.reshape(32, 8, 128))
        level = pot_ref[p][:, None, :] - center
        local = gain * (level * field - 0.5 * total) - prev_ref[p]
        local_send[:, p] = local.reshape(RING, 16, 128).astype(BF)
        return carry

    lax.fori_loop(0, HALO, local_terms, 0)
    local_got[me] = local_send[me]

    for k in (0,) + ORDER:
        source = lax.rem(me - k + RING, RING)
        side, group = source // GROUP, lax.rem(source, GROUP)
        piece = window.at[1 + side, group]
        if k:
            remote(piece, piece, psi_ss.at[k], psi_rs.at[k], at_ring(source)).wait_recv()
        copy = remote(
            piece, window.at[3 - 3 * side, group], halo_ss.at[k], halo_rs.at[k],
            at_column(column + 2 * side - 1),
        )
        copy.start()
        sends.append(copy)

    remote(
        far_proj_ref, proj.at[1 - half, :, inner], proj_ss.at[0], proj_rs.at[0], at_ring(mirror)
    ).wait_recv()
    copy = remote(
        proj.at[1, :, inner], proj_low.at[:, inner], proj_ss.at[1], proj_rs.at[1],
        at_column(column + 1),
    )
    copy.start()
    sends.append(copy)

    for k in ORDER:
        copy = remote(
            local_send.at[ring(k)], local_got.at[me], local_ss.at[k], local_rs.at[k],
            at_ring(ring(k)),
        )
        copy.start()
        sends.append(copy)

    slabs = [lax.rem(2 * column - 1 + k + SLABS, SLABS) for k in range(3)]

    def start(k, a):
        return jnp.clip(planes_ref[slabs[k] * ATOM_DEV + a] - slabs[k] * HALO, 0, HALO - 1)

    starts = [[start(k, a) for a in range(ATOM_DEV)] for k in range(3)]

    def stack(k, plane):
        table = proj.at[k - 1] if k else proj_low
        rows = [table[a, plane - starts[k][a] + PAD] for a in range(ATOM_DEV)]
        return jnp.concatenate(rows, axis=0)

    def psi_plane(m, p):
        return window[m, :, p].reshape(128, 128)

    coef_acc[...] = jnp.zeros_like(coef_acc)

    def coefs(pairs):
        def body(p, carry):
            for m, k in pairs:
                coef_acc[k] += nt_dot(psi_plane(m, p), stack(k, HALO * (m - k) + p))
            return carry

        lax.fori_loop(0, HALO, body, 0)

    coefs(((1, 1), (2, 1), (2, 2)))
    remote(
        proj.at[1, :, inner], proj_low.at[:, inner], proj_ss.at[1], proj_rs.at[1],
        at_column(column - 1),
    ).wait_recv()
    for k in (0,) + ORDER:
        source = lax.rem(me - k + RING, RING)
        side, group = source // GROUP, lax.rem(source, GROUP)
        slot = window.at[3 - 3 * side, group]
        remote(
            slot, slot, halo_ss.at[k], halo_rs.at[k], at_column(column + 2 * side - 1)
        ).wait_recv()
    coefs(((1, 0), (0, 0), (3, 2)))

    lane = lax.broadcasted_iota(jnp.int32, (GROUP, 8, 128), 2)
    even_row = (lane & 16) == 0

    def swap(value):
        up = pltpu.roll(value, 16, 2)
        down = pltpu.roll(value, 112, 2)
        return jnp.where(even_row, down, up)

    folded = []
    for k in range(3):
        parts = coef_acc[k].reshape(GROUP, 2, 8, 128)
        mixed = jnp.where(even_row, parts[:, 0], parts[:, 1])
        folded.append(mixed + swap(mixed))
    coef_send[0:GROUP] = jnp.where(even_row, folded[0], folded[1])
    coef_send[GROUP:] = folded[2]
    coef_got[me] = coef_send[me]
    for k in ORDER:
        copy = remote(
            coef_send.at[ring(k)], coef_got.at[me], red_ss.at[k], red_rs.at[k], at_ring(ring(k))
        )
        copy.start()
        sends.append(copy)

    def stencil_x(group, carry):
        planes = window[:, group].reshape(24, 16, 128).astype(F32)
        total = jnp.zeros((12, 16, 128), F32)
        for m in range(1, HALO + 1):
            pair = planes[HALO - m : 18 - m] + planes[HALO + m : 18 + m]
            total = total + (-0.5 * gain * stencil_weights[m]) * pair
        along_x[group] = total
        return carry

    lax.fori_loop(0, GROUP, stencil_x, 0)

    for k in ORDER:
        slot = coef_got.at[lax.rem(me - k + RING, RING)]
        remote(slot, slot, red_ss.at[k], red_rs.at[k], at_ring(ring(k))).wait_recv()
    mine = jnp.sum(coef_got[...], axis=0)
    coef_mine[...] = mine
    coef_all[me] = mine
    for k in ORDER:
        copy = remote(coef_mine, coef_all.at[me], all_ss.at[k], all_rs.at[k], at_ring(ring(k)))
        copy.start()
        sends.append(copy)
    gram_acc[...] = jnp.zeros_like(gram_acc)
    for k in ORDER:
        slot = coef_all.at[lax.rem(me - k + RING, RING)]
        remote(coef_mine, slot, all_ss.at[k], all_rs.at[k], at_ring(ring(k))).wait_recv()

    shared = coef_all[0:GROUP]
    crossed = swap(shared)
    full = [
        jnp.where(even_row, shared, crossed),
        jnp.where(even_row, crossed, shared),
        coef_all[GROUP:],
    ]
    weights = []
    for k in range(3):
        weighted = full[k] * (gain * strength_ref[pl.ds(slabs[k], 1)])
        rows = [jnp.where(even_row, weighted, 0.0), jnp.where(even_row, 0.0, weighted)]
        weights.append(jnp.stack(rows, axis=1).reshape(128, 128).astype(BF))

    for k in ORDER:
        slot = local_got.at[lax.rem(me - k + RING, RING)]
        remote(slot, slot, local_ss.at[k], local_rs.at[k], at_ring(ring(k))).wait_recv()

    for m in (1, 2):
        side = m - 1
        both = jnp.concatenate([weights[m - 1], weights[m]], axis=1)
        rows = pl.ds(side * GROUP, GROUP)

        def finish(p, carry):
            table = jnp.concatenate([stack(m - 1, HALO + p), stack(m, p)], axis=0)
            term = jnp.dot(both, table, preferred_element_type=F32)
            term = term + along_x[:, side * HALO + p].reshape(128, 128)
            term = term + local_got[rows, p].reshape(128, 128).astype(F32)
            value = term.astype(BF)
            filt_send[rows, p] = value.reshape(GROUP, 16, 128)
            columns = jnp.concatenate([value, psi_plane(m, p)], axis=0)
            gram_acc[...] += nt_dot(value, columns)
            return carry

        lax.fori_loop(0, HALO, finish, 0)
        for k in ORDER:
            target = ring(k)

            @pl.when(target // GROUP == side)
            def _():
                remote(
                    filt_send.at[target], filtered_ref.at[me], filt_ss.at[k], filt_rs.at[k],
                    at_ring(target),
                ).start()

    filtered_ref[me] = filt_send[me]

    even_eight = (lane & 8) == 0
    parts = gram_acc[...].reshape(GROUP, 2, 8, 256)
    left = jnp.where(even_eight, parts[:, 0, :, :128], parts[:, 1, :, :128])
    right = jnp.where(even_eight, parts[:, 0, :, 128:], parts[:, 1, :, 128:])
    merged = jnp.where(
        even_eight, left + pltpu.roll(left, 120, 2), right + pltpu.roll(right, 8, 2)
    )
    gram_y_send[...] = merged.reshape(SIDE, 16, 128)
    gram_y_got[col_y] = gram_y_send[col_y]
    for k in (1, 3, 2):
        to = lax.rem(col_y + k, SIDE)
        copy = remote(
            gram_y_send.at[to], gram_y_got.at[col_y], gy_ss.at[k], gy_rs.at[k],
            at_column(to * SIDE + col_x),
        )
        copy.start()
        sends.append(copy)
    for k in (1, 3, 2):
        source = lax.rem(col_y - k + SIDE, SIDE)
        slot = gram_y_got.at[source]
        remote(
            slot, slot, gy_ss.at[k], gy_rs.at[k], at_column(source * SIDE + col_x)
        ).wait_recv()
    rows_y = jnp.sum(gram_y_got[...], axis=0)
    for x in range(SIDE):
        block = rows_y[4 * x : 4 * x + 4]
        gram_x_send[x] = jnp.concatenate([block, jnp.zeros((4, 128), F32)], axis=0)
    gram_x_got[col_x] = gram_x_send[col_x]
    for k in (1, 3, 2):
        to = lax.rem(col_x + k, SIDE)
        copy = remote(
            gram_x_send.at[to], gram_x_got.at[col_x], gx_ss.at[k], gx_rs.at[k],
            at_column(col_y * SIDE + to),
        )
        copy.start()
        sends.append(copy)
    for k in (1, 3, 2):
        source = lax.rem(col_x - k + SIDE, SIDE)
        slot = gram_x_got.at[source]
        remote(
            slot, slot, gx_ss.at[k], gx_rs.at[k], at_column(col_y * SIDE + source)
        ).wait_recv()
    rows_x = jnp.sum(gram_x_got[...], axis=0)
    gram_z_send[...] = rows_x
    gram_z_got[me] = rows_x
    for k in ORDER:
        copy = remote(gram_z_send, gram_z_got.at[me], gz_ss.at[k], gz_rs.at[k], at_ring(ring(k)))
        copy.start()
        sends.append(copy)
    for k in ORDER:
        slot = gram_z_got.at[lax.rem(me - k + RING, RING)]
        remote(gram_z_send, slot, gz_ss.at[k], gz_rs.at[k], at_ring(ring(k))).wait_recv()
    gram_ref[...] = jnp.sum(gram_z_got[...], axis=0) * scale

    for k in ORDER:
        copy = remote(
            filt_send.at[ring(k)], filtered_ref.at[lax.rem(me - k + RING, RING)],
            filt_ss.at[k], filt_rs.at[k], at_ring(ring(k)),
        )
        copy.wait_recv()
        copy.wait_send()
    for copy in sends:
        copy.wait_send()


def shards(orbitals, previous, potential, projectors, strengths, atom_planes):
    band_dev, slab_planes, cells_y, cells_z = orbitals.shape
    space_count, band_count = lax.axis_size("space"), lax.axis_size("band")
    cells = slab_planes * space_count * cells_y * cells_z
    half = lax.rem(lax.axis_index("space"), 2)
    band = lax.axis_index("band")
    own = half * GROUP + band
    far = (1 - half) * GROUP + (3 - band // 2) * 2 + lax.rem(band, 2)

    def rows_of(pair):
        piece = lax.dynamic_slice_in_dim(projectors, 2 * pair, 2, 3)
        piece = piece.transpose(0, 2, 3, 1, 4)
        piece = jnp.pad(piece, ((0, 0), (0, 0), (0, 0), (0, 16 - NPJ), (0, 0)))
        return piece.reshape(ATOM_DEV, BOX, 32, cells_z)

    levels = strengths.reshape(SLABS, ATOM_DEV, 1, NPJ)
    levels = jnp.pad(levels, ((0, 0), (0, 0), (0, 0), (0, 16 - NPJ)))
    levels = jnp.broadcast_to(levels, (SLABS, ATOM_DEV, 2, 16)).reshape(SLABS, 128)

    vmem = pl.BlockSpec(memory_space=pltpu.VMEM)
    dma = pltpu.SemaphoreType.DMA
    slab_rows = (RING, HALO, 16, 128)
    tile = (8, 128)
    sems = [RING, RING, RING, RING, 2, 2] + [RING] * 8 + [SIDE] * 4 + [RING] * 2
    filtered, gram = pl.pallas_call(
        lambda *refs: step_kernel(1.0 / cells, *refs),
        out_shape=(
            jax.ShapeDtypeStruct(slab_rows, BF),
            jax.ShapeDtypeStruct(tile, F32),
        ),
        in_specs=[pl.BlockSpec(memory_space=pltpu.SMEM)] + [vmem] * 6,
        out_specs=(vmem, vmem),
        scratch_shapes=[
            pltpu.VMEM(slab_rows, BF),
            pltpu.VMEM(slab_rows, BF),
            pltpu.VMEM((4, GROUP, HALO, 16, 128), BF),
            pltpu.VMEM(slab_rows, BF),
            pltpu.VMEM(slab_rows, BF),
            pltpu.VMEM((2, ATOM_DEV, PAD + 2 * BOX, 32, 128), BF),
            pltpu.VMEM((ATOM_DEV, PAD + 2 * BOX, 32, 128), BF),
            pltpu.VMEM((GROUP, 12, 16, 128), F32),
            pltpu.VMEM((3, 128, 128), F32),
            pltpu.VMEM((RING,) + tile, F32),
            pltpu.VMEM((RING,) + tile, F32),
            pltpu.VMEM(tile, F32),
            pltpu.VMEM((RING,) + tile, F32),
            pltpu.VMEM((128, 256), F32),
            pltpu.VMEM((SIDE, 16, 128), F32),
            pltpu.VMEM((SIDE, 16, 128), F32),
            pltpu.VMEM((SIDE,) + tile, F32),
            pltpu.VMEM((SIDE,) + tile, F32),
            pltpu.VMEM(tile, F32),
            pltpu.VMEM((RING,) + tile, F32),
        ]
        + [dma((n,)) for n in sems],
        compiler_params=pltpu.CompilerParams(
            collective_id=0, has_side_effects=True, vmem_limit_bytes=50 << 20
        ),
        name="filter_step",
    )(
        atom_planes,
        orbitals.transpose(1, 2, 0, 3),
        previous.transpose(1, 2, 0, 3),
        potential,
        rows_of(own),
        rows_of(far),
        levels,
    )
    filtered = filtered.reshape(RING, HALO, 2, band_dev, cells_z)
    filtered = filtered.transpose(3, 1, 0, 2, 4).reshape(orbitals.shape)
    gram = gram[:4].reshape(2, 2, GROUP, 2, 8)
    gram = lax.dynamic_index_in_dim(gram, half, 0, keepdims=False)
    gram = lax.dynamic_index_in_dim(gram, band, 1, keepdims=False)
    return filtered, gram[:, 0], gram[:, 1]


def solution(mesh):
    in_specs = (
        P("band", "space", None, None),
        P("band", "space", None, None),
        P("space", None, None),
        P("space", None, None, None, None),
        P(),
        P(),
    )
    out_specs = (P("band", "space", None, None), P("space", "band"), P("space", "band"))
    return jax.shard_map(
        shards, mesh=mesh, in_specs=in_specs, out_specs=out_specs, check_vma=False
    )
```

```python
import jax
import jax.numpy as jnp
from jax import lax
from jax.experimental import pallas as pl
from jax.experimental.pallas import tpu as pltpu
from jax.sharding import PartitionSpec as P

MESH = pl.DeviceIdType.MESH
BF = jnp.bfloat16
F32 = jnp.float32

HALO = 6
BOX = 6
NPJ = 9
ATOM_DEV = 4
RING = 16
GROUP = 8
COLUMNS = 16
SLABS = 32
PAD = BOX - 1
ROWS = 2 * BOX * NPJ
WINDOWS = (0, 96, 208, 304)
ORDER = (1, 15, 2, 14, 3, 13, 4, 12, 5, 11, 6, 10, 7, 9, 8)

stencil_weights = (
    -5369.0 / 1800.0,
    12.0 / 7.0,
    -15.0 / 56.0,
    10.0 / 189.0,
    -1.0 / 112.0,
    2.0 / 1925.0,
    -1.0 / 16632.0,
)
center = 5.5
halfwidth = 5.5
gain = 2.0 / halfwidth


def nt_dot(a, b):
    return lax.dot_general(a, b, (((1,), (1,)), ((), ())), preferred_element_type=F32)


def step_kernel(
    scale,
    planes_ref,
    psi_ref,
    prev_ref,
    pot_ref,
    own_rows_ref,
    far_rows_ref,
    strength_ref,
    filtered_ref,
    gram_ref,
    psi_send,
    local_send,
    window,
    local_got,
    filt_send,
    proj,
    proj_low,
    far_got,
    low_got,
    spread,
    along_x,
    coef_send,
    coef_got,
    coef_mine,
    coef_all,
    gram_xy_send,
    gram_xy_got,
    gram_z_send,
    gram_z_got,
    psi_ss,
    psi_rs,
    halo_ss,
    halo_rs,
    proj_ss,
    proj_rs,
    local_ss,
    local_rs,
    red_ss,
    red_rs,
    all_ss,
    all_rs,
    filt_ss,
    filt_rs,
    gxy_ss,
    gxy_rs,
    gz_ss,
    gz_rs,
):
    space = lax.axis_index("space")
    band = lax.axis_index("band")
    column, half = space // 2, lax.rem(space, 2)
    me = half * GROUP + band

    def ring(k):
        return lax.rem(me + k, RING)

    def at_ring(index):
        return {"space": column * 2 + index // GROUP, "band": lax.rem(index, GROUP)}

    def at_column(col):
        return {"space": lax.rem(col + COLUMNS, COLUMNS) * 2 + half, "band": band}

    def remote(src, dst, ssem, rsem, device):
        return pltpu.make_async_remote_copy(
            src_ref=src, dst_ref=dst, send_sem=ssem, recv_sem=rsem,
            device_id=device, device_id_type=MESH,
        )

    mirror = (1 - half) * GROUP + (3 - band // 2) * 2 + lax.rem(band, 2)

    barrier = pltpu.get_barrier_semaphore()
    peers = [at_ring(ring(k)) for k in ORDER]
    peers += [at_column(column + k) for k in ORDER]
    for peer in peers:
        pl.semaphore_signal(barrier, inc=1, device_id=peer, device_id_type=MESH)

    def pack(p, carry):
        psi_send[:, p] = psi_ref[p].reshape(RING, 16, 128).astype(BF)
        return carry

    lax.fori_loop(0, HALO, pack, 0)
    for k in range(3):
        table = proj.at[k - 1] if k else proj_low
        table[:, 0:PAD] = jnp.zeros((ATOM_DEV, PAD, 32, 128), BF)
        table[:, PAD + BOX :] = jnp.zeros((ATOM_DEV, BOX, 32, 128), BF)

    row = lax.broadcasted_iota(jnp.int32, (192, 128), 0)
    source_row = lax.broadcasted_iota(jnp.int32, (192, 128), 1) - 12 * (row & 15) - (row >> 4)
    for a in range(ATOM_DEV):
        hit = (source_row == ROWS * a - WINDOWS[a]) & ((row & 15) < NPJ)
        spread[a] = jnp.where(hit, 1.0, 0.0).astype(BF)

    def expand(rows_ref, table):
        for a in range(ATOM_DEV):
            rows = rows_ref[WINDOWS[a] : WINDOWS[a] + 128]
            moved = jnp.dot(spread[a], rows, preferred_element_type=F32)
            table[a, PAD : PAD + BOX] = moved.astype(BF).reshape(BOX, 32, 128)

    expand(own_rows_ref, proj.at[half])
    window[1 + half, band] = psi_send[me]

    pl.semaphore_wait(barrier, len(peers))

    sends = []
    far_copy = remote(far_rows_ref, far_got, proj_ss.at[0], proj_rs.at[0], at_ring(mirror))
    far_copy.start()
    sends.append(far_copy)

    def low_copy(rows_ref, col):
        return remote(rows_ref, low_got, proj_ss.at[1], proj_rs.at[1], at_column(col))

    @pl.when(half == 1)
    def _():
        low_copy(own_rows_ref, column + 1).start()

    for k in ORDER:
        copy = remote(
            psi_send.at[ring(k)], window.at[1 + half, band], psi_ss.at[k], psi_rs.at[k],
            at_ring(ring(k)),
        )
        copy.start()
        sends.append(copy)

    def local_terms(p, carry):
        field = psi_ref[p]
        flat = field.reshape(256, 128)
        total = (3.0 * stencil_weights[0]) * field
        for m in range(1, HALO + 1):
            ahead = jnp.concatenate([field[m:], field[:m]], axis=0)
            behind = jnp.concatenate([field[32 - m :], field[: 32 - m]], axis=0)
            turned = pltpu.roll(flat, m, 1) + pltpu.roll(flat, 128 - m, 1)
            total = total + stencil_weights[m] * (ahead + behind + turned.reshape(32, 8, 128))
        level = pot_ref[p][:, None, :] - center
        local = gain * (level * field - 0.5 * total) - prev_ref[p]
        local_send[:, p] = local.reshape(RING, 16, 128).astype(BF)
        return carry

    lax.fori_loop(0, HALO, local_terms, 0)
    local_got[me] = local_send[me]

    far_copy.wait_recv()

    @pl.when(half == 0)
    def _():
        low_copy(far_got, column + 1).start()

    for k in (0,) + ORDER:
        source = lax.rem(me - k + RING, RING)
        side, group = source // GROUP, lax.rem(source, GROUP)
        piece = window.at[1 + side, group]
        if k:
            remote(piece, piece, psi_ss.at[k], psi_rs.at[k], at_ring(source)).wait_recv()
        copy = remote(
            piece, window.at[3 - 3 * side, group], halo_ss.at[k], halo_rs.at[k],
            at_column(column + 2 * side - 1),
        )
        copy.start()
        sends.append(copy)

    for k in ORDER:
        copy = remote(
            local_send.at[ring(k)], local_got.at[me], local_ss.at[k], local_rs.at[k],
            at_ring(ring(k)),
        )
        copy.start()
        sends.append(copy)

    slabs = [lax.rem(2 * column - 1 + k + SLABS, SLABS) for k in range(3)]

    def start(k, a):
        return jnp.clip(planes_ref[slabs[k] * ATOM_DEV + a] - slabs[k] * HALO, 0, HALO - 1)

    starts = [[start(k, a) for a in range(ATOM_DEV)] for k in range(3)]

    def stack(k, plane):
        table = proj.at[k - 1] if k else proj_low
        rows = [table[a, plane - starts[k][a] + PAD] for a in range(ATOM_DEV)]
        return jnp.concatenate(rows, axis=0)

    def psi_plane(m, p):
        return window[m, :, p].reshape(128, 128)

    def psi_lanes(m):
        return jnp.concatenate([psi_plane(m, p) for p in range(HALO)], axis=1)

    def stack_lanes(k, first):
        return jnp.concatenate([stack(k, first + p) for p in range(HALO)], axis=1)

    expand(far_got, proj.at[1 - half])
    coef_mid = nt_dot(psi_lanes(1), stack_lanes(1, 0)) + nt_dot(psi_lanes(2), stack_lanes(1, HALO))
    coef_high = nt_dot(psi_lanes(2), stack_lanes(2, 0))
    low_copy(far_got, column - 1).wait_recv()
    expand(low_got, proj_low)
    coef_low = nt_dot(psi_lanes(1), stack_lanes(0, HALO))
    for k in (0,) + ORDER:
        source = lax.rem(me - k + RING, RING)
        side, group = source // GROUP, lax.rem(source, GROUP)
        slot = window.at[3 - 3 * side, group]
        remote(
            slot, slot, halo_ss.at[k], halo_rs.at[k], at_column(column + 2 * side - 1)
        ).wait_recv()
    coef_low = coef_low + nt_dot(psi_lanes(0), stack_lanes(0, 0))
    coef_high = coef_high + nt_dot(psi_lanes(3), stack_lanes(2, HALO))

    lane = lax.broadcasted_iota(jnp.int32, (GROUP, 8, 128), 2)
    even_row = (lane & 16) == 0

    def swap(value):
        up = pltpu.roll(value, 16, 2)
        down = pltpu.roll(value, 112, 2)
        return jnp.where(even_row, down, up)

    folded = []
    for coef in (coef_low, coef_mid, coef_high):
        parts = coef.reshape(GROUP, 2, 8, 128)
        mixed = jnp.where(even_row, parts[:, 0], parts[:, 1])
        folded.append(mixed + swap(mixed))
    coef_send[0:GROUP] = jnp.where(even_row, folded[0], folded[1])
    coef_send[GROUP:] = folded[2]
    coef_got[me] = coef_send[me]
    for k in ORDER:
        copy = remote(
            coef_send.at[ring(k)], coef_got.at[me], red_ss.at[k], red_rs.at[k], at_ring(ring(k))
        )
        copy.start()
        sends.append(copy)

    def stencil_x(group, carry):
        planes = window[:, group].reshape(24, 16, 128).astype(F32)
        total = jnp.zeros((12, 16, 128), F32)
        for m in range(1, HALO + 1):
            pair = planes[HALO - m : 18 - m] + planes[HALO + m : 18 + m]
            total = total + (-0.5 * gain * stencil_weights[m]) * pair
        along_x[group] = total
        return carry

    lax.fori_loop(0, GROUP, stencil_x, 0)

    for k in ORDER:
        slot = coef_got.at[lax.rem(me - k + RING, RING)]
        remote(slot, slot, red_ss.at[k], red_rs.at[k], at_ring(ring(k))).wait_recv()
    mine = jnp.sum(coef_got[...], axis=0)
    coef_mine[...] = mine
    coef_all[me] = mine
    for k in ORDER:
        copy = remote(coef_mine, coef_all.at[me], all_ss.at[k], all_rs.at[k], at_ring(ring(k)))
        copy.start()
        sends.append(copy)
    for k in ORDER:
        slot = coef_all.at[lax.rem(me - k + RING, RING)]
        remote(coef_mine, slot, all_ss.at[k], all_rs.at[k], at_ring(ring(k))).wait_recv()

    shared = coef_all[0:GROUP]
    crossed = swap(shared)
    full = [
        jnp.where(even_row, shared, crossed),
        jnp.where(even_row, crossed, shared),
        coef_all[GROUP:],
    ]
    weights = []
    for k in range(3):
        weighted = full[k] * (gain * strength_ref[pl.ds(slabs[k], 1)])
        rows = [jnp.where(even_row, weighted, 0.0), jnp.where(even_row, 0.0, weighted)]
        weights.append(jnp.stack(rows, axis=1).reshape(128, 128).astype(BF))

    for k in ORDER:
        slot = local_got.at[lax.rem(me - k + RING, RING)]
        remote(slot, slot, local_ss.at[k], local_rs.at[k], at_ring(ring(k))).wait_recv()

    gram = jnp.zeros((128, 256), F32)
    for m in (1, 2):
        side = m - 1
        both = jnp.concatenate([weights[m - 1], weights[m]], axis=1)
        rows = pl.ds(side * GROUP, GROUP)

        values = []
        for p in range(HALO):
            table = jnp.concatenate([stack(m - 1, HALO + p), stack(m, p)], axis=0)
            term = jnp.dot(both, table, preferred_element_type=F32)
            term = term + along_x[:, side * HALO + p].reshape(128, 128)
            term = term + local_got[rows, p].reshape(128, 128).astype(F32)
            values.append(term.astype(BF))
            filt_send[rows, p] = values[p].reshape(GROUP, 16, 128)
        for k in ORDER:
            target = ring(k)

            @pl.when(target // GROUP == side)
            def _():
                remote(
                    filt_send.at[target], filtered_ref.at[me], filt_ss.at[k], filt_rs.at[k],
                    at_ring(target),
                ).start()

        value = jnp.concatenate(values, axis=1)
        gram = gram + nt_dot(value, jnp.concatenate([value, psi_lanes(m)], axis=0))

    filtered_ref[me] = filt_send[me]

    even_eight = (lane & 8) == 0
    parts = gram.reshape(GROUP, 2, 8, 256)
    left = jnp.where(even_eight, parts[:, 0, :, :128], parts[:, 1, :, :128])
    right = jnp.where(even_eight, parts[:, 0, :, 128:], parts[:, 1, :, 128:])
    merged = jnp.where(
        even_eight, left + pltpu.roll(left, 120, 2), right + pltpu.roll(right, 8, 2)
    )
    merged = merged.reshape(64, 128)
    for c in range(COLUMNS):
        block = merged[4 * c : 4 * c + 4]
        gram_xy_send[c] = jnp.concatenate([block, jnp.zeros((4, 128), F32)], axis=0)
    gram_xy_got[column] = gram_xy_send[column]
    for k in ORDER:
        to = lax.rem(column + k, COLUMNS)
        copy = remote(
            gram_xy_send.at[to], gram_xy_got.at[column], gxy_ss.at[k], gxy_rs.at[k], at_column(to)
        )
        copy.start()
        sends.append(copy)
    for k in ORDER:
        source = lax.rem(column - k + COLUMNS, COLUMNS)
        slot = gram_xy_got.at[source]
        remote(slot, slot, gxy_ss.at[k], gxy_rs.at[k], at_column(source)).wait_recv()
    rows_x = jnp.sum(gram_xy_got[...], axis=0)
    gram_z_send[...] = rows_x
    gram_z_got[me] = rows_x
    for k in ORDER:
        copy = remote(gram_z_send, gram_z_got.at[me], gz_ss.at[k], gz_rs.at[k], at_ring(ring(k)))
        copy.start()
        sends.append(copy)
    for k in ORDER:
        slot = gram_z_got.at[lax.rem(me - k + RING, RING)]
        remote(gram_z_send, slot, gz_ss.at[k], gz_rs.at[k], at_ring(ring(k))).wait_recv()
    gram_ref[...] = jnp.sum(gram_z_got[...], axis=0) * scale

    for k in ORDER:
        copy = remote(
            filt_send.at[ring(k)], filtered_ref.at[lax.rem(me - k + RING, RING)],
            filt_ss.at[k], filt_rs.at[k], at_ring(ring(k)),
        )
        copy.wait_recv()
        copy.wait_send()
    low_copy(far_got, column + 1).wait_send()
    for copy in sends:
        copy.wait_send()


def shards(orbitals, previous, potential, projectors, strengths, atom_planes):
    band_dev, slab_planes, cells_y, cells_z = orbitals.shape
    space_count, band_count = lax.axis_size("space"), lax.axis_size("band")
    cells = slab_planes * space_count * cells_y * cells_z
    half = lax.rem(lax.axis_index("space"), 2)
    band = lax.axis_index("band")
    own = half * GROUP + band
    far = (1 - half) * GROUP + (3 - band // 2) * 2 + lax.rem(band, 2)

    def rows_of(pair):
        piece = lax.dynamic_slice_in_dim(projectors, 2 * pair, 2, 3)
        return piece.reshape(ATOM_DEV * ROWS, cells_z)

    levels = strengths.reshape(SLABS, ATOM_DEV, 1, NPJ)
    levels = jnp.pad(levels, ((0, 0), (0, 0), (0, 0), (0, 16 - NPJ)))
    levels = jnp.broadcast_to(levels, (SLABS, ATOM_DEV, 2, 16)).reshape(SLABS, 128)

    vmem = pl.BlockSpec(memory_space=pltpu.VMEM)
    dma = pltpu.SemaphoreType.DMA
    slab_rows = (RING, HALO, 16, 128)
    tile = (8, 128)
    sems = [RING] * 4 + [2, 2] + [RING] * 12
    filtered, gram = pl.pallas_call(
        lambda *refs: step_kernel(1.0 / cells, *refs),
        out_shape=(
            jax.ShapeDtypeStruct(slab_rows, BF),
            jax.ShapeDtypeStruct(tile, F32),
        ),
        in_specs=[pl.BlockSpec(memory_space=pltpu.SMEM)] + [vmem] * 6,
        out_specs=(vmem, vmem),
        scratch_shapes=[
            pltpu.VMEM(slab_rows, BF),
            pltpu.VMEM(slab_rows, BF),
            pltpu.VMEM((4, GROUP, HALO, 16, 128), BF),
            pltpu.VMEM(slab_rows, BF),
            pltpu.VMEM(slab_rows, BF),
            pltpu.VMEM((2, ATOM_DEV, PAD + 2 * BOX, 32, 128), BF),
            pltpu.VMEM((ATOM_DEV, PAD + 2 * BOX, 32, 128), BF),
            pltpu.VMEM((ATOM_DEV * ROWS, 128), BF),
            pltpu.VMEM((ATOM_DEV * ROWS, 128), BF),
            pltpu.VMEM((ATOM_DEV, 192, 128), BF),
            pltpu.VMEM((GROUP, 12, 16, 128), F32),
            pltpu.VMEM((RING,) + tile, F32),
            pltpu.VMEM((RING,) + tile, F32),
            pltpu.VMEM(tile, F32),
            pltpu.VMEM((RING,) + tile, F32),
            pltpu.VMEM((COLUMNS,) + tile, F32),
            pltpu.VMEM((COLUMNS,) + tile, F32),
            pltpu.VMEM(tile, F32),
            pltpu.VMEM((RING,) + tile, F32),
        ]
        + [dma((n,)) for n in sems],
        compiler_params=pltpu.CompilerParams(
            collective_id=0, has_side_effects=True, vmem_limit_bytes=50 << 20
        ),
        name="filter_step",
    )(
        atom_planes,
        orbitals.transpose(1, 2, 0, 3),
        previous.transpose(1, 2, 0, 3),
        potential,
        rows_of(own),
        rows_of(far),
        levels,
    )
    filtered = filtered.reshape(RING, HALO, 2, band_dev, cells_z)
    filtered = filtered.transpose(3, 1, 0, 2, 4).reshape(orbitals.shape)
    gram = gram[:4].reshape(2, 2, GROUP, 2, 8)
    gram = lax.dynamic_index_in_dim(gram, half, 0, keepdims=False)
    gram = lax.dynamic_index_in_dim(gram, band, 1, keepdims=False)
    return filtered, gram[:, 0], gram[:, 1]


def solution(mesh):
    in_specs = (
        P("band", "space", None, None),
        P("band", "space", None, None),
        P("space", None, None),
        P("space", None, None, None, None),
        P(),
        P(),
    )
    out_specs = (P("band", "space", None, None), P("space", "band"), P("space", "band"))
    return jax.shard_map(
        shards, mesh=mesh, in_specs=in_specs, out_specs=out_specs, check_vma=False
    )
```

```python
import jax
import jax.numpy as jnp
from jax import lax
from jax.experimental import pallas as pl
from jax.experimental.pallas import tpu as pltpu
from jax.sharding import PartitionSpec as P

MESH = pl.DeviceIdType.MESH
BF = jnp.bfloat16
F32 = jnp.float32

HALO = 6
BOX = 6
NPJ = 9
ATOM_DEV = 4
RING = 16
GROUP = 8
COLUMNS = 16
SLABS = 32
PAD = BOX - 1
ROWS = 2 * BOX * NPJ
WINDOWS = (0, 96, 208, 304)
ORDER = (1, 15, 2, 14, 3, 13, 4, 12, 5, 11, 6, 10, 7, 9, 8)

stencil_weights = (
    -5369.0 / 1800.0,
    12.0 / 7.0,
    -15.0 / 56.0,
    10.0 / 189.0,
    -1.0 / 112.0,
    2.0 / 1925.0,
    -1.0 / 16632.0,
)
center = 5.5
halfwidth = 5.5
gain = 2.0 / halfwidth


def nt_dot(a, b):
    return lax.dot_general(a, b, (((1,), (1,)), ((), ())), preferred_element_type=F32)


def step_kernel(
    scale,
    planes_in,
    psi_in,
    prev_in,
    pot_in,
    proj_ref,
    strength_in,
    filtered_ref,
    gram_ref,
    planes_ref,
    psi_ref,
    prev_ref,
    pot_ref,
    strength_ref,
    psi_rows,
    near,
    own_rows,
    far_rows,
    pick,
    psi_send,
    local_send,
    window,
    local_got,
    filt_send,
    proj,
    proj_low,
    far_got,
    low_got,
    spread,
    along_x,
    coef_send,
    coef_got,
    coef_mine,
    coef_all,
    gram_xy_send,
    gram_xy_got,
    gram_z_send,
    gram_z_got,
    load_sem,
    near_sem,
    psi_ss,
    psi_rs,
    halo_ss,
    halo_rs,
    proj_ss,
    proj_rs,
    local_ss,
    local_rs,
    red_ss,
    red_rs,
    all_ss,
    all_rs,
    filt_ss,
    filt_rs,
    gxy_ss,
    gxy_rs,
    gz_ss,
    gz_rs,
):
    space = lax.axis_index("space")
    band = lax.axis_index("band")
    column, half = space // 2, lax.rem(space, 2)
    me = half * GROUP + band

    def ring(k):
        return lax.rem(me + k, RING)

    def at_ring(index):
        return {"space": column * 2 + index // GROUP, "band": lax.rem(index, GROUP)}

    def at_column(col):
        return {"space": lax.rem(col + COLUMNS, COLUMNS) * 2 + half, "band": band}

    def remote(src, dst, ssem, rsem, device):
        return pltpu.make_async_remote_copy(
            src_ref=src, dst_ref=dst, send_sem=ssem, recv_sem=rsem,
            device_id=device, device_id_type=MESH,
        )

    mirror = (1 - half) * GROUP + (3 - band // 2) * 2 + lax.rem(band, 2)

    barrier = pltpu.get_barrier_semaphore()
    peers = [at_ring(ring(k)) for k in ORDER]
    peers += [at_column(column + k) for k in ORDER]
    for peer in peers:
        pl.semaphore_signal(barrier, inc=1, device_id=peer, device_id_type=MESH)

    loads = [
        pltpu.make_async_copy(source, target, load_sem.at[i])
        for i, (source, target) in enumerate(
            (
                (psi_in, psi_ref),
                (strength_in, strength_ref),
                (planes_in, planes_ref),
                (pot_in, pot_ref),
                (prev_in, prev_ref),
            )
        )
    ]
    loads[0].start()

    fetches = []
    for i, pair in enumerate((me, mirror)):
        block = pl.ds(pl.multiple_of(pair // 4 * 8, 8), 8)
        fetch = pltpu.make_async_copy(proj_ref.at[:, :, :, block, :], near.at[i], near_sem.at[i])
        fetch.start()
        fetches.append(fetch)
    for load in loads[1:]:
        load.start()
    loads[0].wait()

    def pack(p, carry):
        turned = jnp.swapaxes(psi_ref[:, p], 0, 1)
        psi_rows[p] = turned
        psi_send[:, p] = turned.reshape(RING, 16, 128).astype(BF)
        return carry

    lax.fori_loop(0, HALO, pack, 0)
    for k in range(3):
        table = proj.at[k - 1] if k else proj_low
        table[:, 0:PAD] = jnp.zeros((ATOM_DEV, PAD, 32, 128), BF)
        table[:, PAD + BOX :] = jnp.zeros((ATOM_DEV, BOX, 32, 128), BF)

    row = lax.broadcasted_iota(jnp.int32, (192, 128), 0)
    source_row = lax.broadcasted_iota(jnp.int32, (192, 128), 1) - 12 * (row & 15) - (row >> 4)
    for a in range(ATOM_DEV):
        hit = (source_row == ROWS * a - WINDOWS[a]) & ((row & 15) < NPJ)
        spread[a] = jnp.where(hit, 1.0, 0.0).astype(BF)

    def expand(rows_ref, table):
        for a in range(ATOM_DEV):
            rows = rows_ref[WINDOWS[a] : WINDOWS[a] + 128]
            moved = jnp.dot(spread[a], rows, preferred_element_type=F32)
            table[a, PAD : PAD + BOX] = moved.astype(BF).reshape(BOX, 32, 128)

    pick_row = lax.broadcasted_iota(jnp.int32, (32, 128), 0)
    pick_from = lax.broadcasted_iota(jnp.int32, (32, 128), 1)
    for i, (pair, rows_ref) in enumerate(((mirror, far_rows), (me, own_rows))):
        wanted = 8 * (pick_row >> 1) + 2 * lax.rem(pair, 4) + (pick_row & 1)
        pick[i] = jnp.where(pick_from == wanted, 1.0, 0.0).astype(BF)
        fetches[1 - i].wait()
        flat = near[1 - i].reshape(ATOM_DEV * ROWS * 4, 128)
        for g in range(14):
            first = min(128 * g, ATOM_DEV * ROWS * 4 - 128)
            rows = jnp.dot(pick[i], flat[first : first + 128], preferred_element_type=F32)
            rows_ref[first // 4 : first // 4 + 32] = rows.astype(BF)

    expand(own_rows, proj.at[half])

    loads[1].wait()
    loads[2].wait()
    lane_row = lax.broadcasted_iota(jnp.int32, (128, 128), 0)
    lane_col = lax.broadcasted_iota(jnp.int32, (128, 128), 1)
    own_lane = lax.broadcasted_iota(jnp.int32, (NPJ, 128), 0)
    own_lane = own_lane == (lax.broadcasted_iota(jnp.int32, (NPJ, 128), 1) & 15)
    slabs = [lax.rem(2 * column - 1 + k + SLABS, SLABS) for k in range(3)]
    levels = []
    for k in range(3):
        take = jnp.where(lane_row == slabs[k] * ATOM_DEV + (lane_col >> 5), 1.0, 0.0)
        spread_levels = jnp.dot(
            strength_ref[...], take, precision=lax.Precision.HIGHEST, preferred_element_type=F32
        )
        picked = jnp.where(own_lane, spread_levels, 0.0)
        levels.append(gain * jnp.sum(picked, axis=0, keepdims=True))
    window[1 + half, band] = psi_send[me]

    pl.semaphore_wait(barrier, len(peers))

    sends = []
    far_copy = remote(far_rows, far_got, proj_ss.at[0], proj_rs.at[0], at_ring(mirror))
    far_copy.start()
    sends.append(far_copy)

    def low_copy(rows_ref, col):
        return remote(rows_ref, low_got, proj_ss.at[1], proj_rs.at[1], at_column(col))

    @pl.when(half == 1)
    def _():
        low_copy(own_rows, column + 1).start()

    for k in ORDER:
        copy = remote(
            psi_send.at[ring(k)], window.at[1 + half, band], psi_ss.at[k], psi_rs.at[k],
            at_ring(ring(k)),
        )
        copy.start()
        sends.append(copy)

    loads[3].wait()
    loads[4].wait()
    def local_terms(p, carry):
        field = psi_rows[p]
        flat = field.reshape(256, 128)
        total = (3.0 * stencil_weights[0]) * field
        for m in range(1, HALO + 1):
            ahead = jnp.concatenate([field[m:], field[:m]], axis=0)
            behind = jnp.concatenate([field[32 - m :], field[: 32 - m]], axis=0)
            turned = pltpu.roll(flat, m, 1) + pltpu.roll(flat, 128 - m, 1)
            total = total + stencil_weights[m] * (ahead + behind + turned.reshape(32, 8, 128))
        level = pot_ref[p][:, None, :] - center
        local = gain * (level * field - 0.5 * total) - jnp.swapaxes(prev_ref[:, p], 0, 1)
        local_send[:, p] = local.reshape(RING, 16, 128).astype(BF)
        return carry

    lax.fori_loop(0, HALO, local_terms, 0)
    local_got[me] = local_send[me]

    far_copy.wait_recv()

    @pl.when(half == 0)
    def _():
        low_copy(far_got, column + 1).start()

    for k in (0,) + ORDER:
        source = lax.rem(me - k + RING, RING)
        side, group = source // GROUP, lax.rem(source, GROUP)
        piece = window.at[1 + side, group]
        if k:
            remote(piece, piece, psi_ss.at[k], psi_rs.at[k], at_ring(source)).wait_recv()
        copy = remote(
            piece, window.at[3 - 3 * side, group], halo_ss.at[k], halo_rs.at[k],
            at_column(column + 2 * side - 1),
        )
        copy.start()
        sends.append(copy)

    for k in ORDER:
        copy = remote(
            local_send.at[ring(k)], local_got.at[me], local_ss.at[k], local_rs.at[k],
            at_ring(ring(k)),
        )
        copy.start()
        sends.append(copy)

    def start(k, a):
        return jnp.clip(planes_ref[slabs[k] * ATOM_DEV + a] - slabs[k] * HALO, 0, HALO - 1)

    starts = [[start(k, a) for a in range(ATOM_DEV)] for k in range(3)]

    def stack(k, plane):
        table = proj.at[k - 1] if k else proj_low
        rows = [table[a, plane - starts[k][a] + PAD] for a in range(ATOM_DEV)]
        return jnp.concatenate(rows, axis=0)

    def psi_plane(m, p):
        return window[m, :, p].reshape(128, 128)

    def psi_lanes(m):
        return jnp.concatenate([psi_plane(m, p) for p in range(HALO)], axis=1)

    def stack_lanes(k, first):
        return jnp.concatenate([stack(k, first + p) for p in range(HALO)], axis=1)

    expand(far_got, proj.at[1 - half])
    coef_mid = nt_dot(psi_lanes(1), stack_lanes(1, 0)) + nt_dot(psi_lanes(2), stack_lanes(1, HALO))
    coef_high = nt_dot(psi_lanes(2), stack_lanes(2, 0))
    low_copy(far_got, column - 1).wait_recv()
    expand(low_got, proj_low)
    coef_low = nt_dot(psi_lanes(1), stack_lanes(0, HALO))
    for k in (0,) + ORDER:
        source = lax.rem(me - k + RING, RING)
        side, group = source // GROUP, lax.rem(source, GROUP)
        slot = window.at[3 - 3 * side, group]
        remote(
            slot, slot, halo_ss.at[k], halo_rs.at[k], at_column(column + 2 * side - 1)
        ).wait_recv()
    coef_low = coef_low + nt_dot(psi_lanes(0), stack_lanes(0, 0))
    coef_high = coef_high + nt_dot(psi_lanes(3), stack_lanes(2, HALO))

    lane = lax.broadcasted_iota(jnp.int32, (GROUP, 8, 128), 2)
    even_row = (lane & 16) == 0

    def swap(value):
        up = pltpu.roll(value, 16, 2)
        down = pltpu.roll(value, 112, 2)
        return jnp.where(even_row, down, up)

    folded = []
    for coef in (coef_low, coef_mid, coef_high):
        parts = coef.reshape(GROUP, 2, 8, 128)
        mixed = jnp.where(even_row, parts[:, 0], parts[:, 1])
        folded.append(mixed + swap(mixed))
    coef_send[0:GROUP] = jnp.where(even_row, folded[0], folded[1])
    coef_send[GROUP:] = folded[2]
    coef_got[me] = coef_send[me]
    for k in ORDER:
        copy = remote(
            coef_send.at[ring(k)], coef_got.at[me], red_ss.at[k], red_rs.at[k], at_ring(ring(k))
        )
        copy.start()
        sends.append(copy)

    def stencil_x(group, carry):
        planes = window[:, group].reshape(24, 16, 128).astype(F32)
        total = jnp.zeros((12, 16, 128), F32)
        for m in range(1, HALO + 1):
            pair = planes[HALO - m : 18 - m] + planes[HALO + m : 18 + m]
            total = total + (-0.5 * gain * stencil_weights[m]) * pair
        along_x[group] = total
        return carry

    lax.fori_loop(0, GROUP, stencil_x, 0)

    for k in ORDER:
        slot = coef_got.at[lax.rem(me - k + RING, RING)]
        remote(slot, slot, red_ss.at[k], red_rs.at[k], at_ring(ring(k))).wait_recv()
    mine = jnp.sum(coef_got[...], axis=0)
    coef_mine[...] = mine
    coef_all[me] = mine
    for k in ORDER:
        copy = remote(coef_mine, coef_all.at[me], all_ss.at[k], all_rs.at[k], at_ring(ring(k)))
        copy.start()
        sends.append(copy)
    for k in ORDER:
        slot = coef_all.at[lax.rem(me - k + RING, RING)]
        remote(coef_mine, slot, all_ss.at[k], all_rs.at[k], at_ring(ring(k))).wait_recv()

    shared = coef_all[0:GROUP]
    crossed = swap(shared)
    full = [
        jnp.where(even_row, shared, crossed),
        jnp.where(even_row, crossed, shared),
        coef_all[GROUP:],
    ]
    weights = []
    for k in range(3):
        weighted = full[k] * levels[k]
        rows = [jnp.where(even_row, weighted, 0.0), jnp.where(even_row, 0.0, weighted)]
        weights.append(jnp.stack(rows, axis=1).reshape(128, 128).astype(BF))

    for k in ORDER:
        slot = local_got.at[lax.rem(me - k + RING, RING)]
        remote(slot, slot, local_ss.at[k], local_rs.at[k], at_ring(ring(k))).wait_recv()

    gram = jnp.zeros((128, 256), F32)
    for m in (1, 2):
        side = m - 1
        both = jnp.concatenate([weights[m - 1], weights[m]], axis=1)
        rows = pl.ds(side * GROUP, GROUP)

        values = []
        for p in range(HALO):
            table = jnp.concatenate([stack(m - 1, HALO + p), stack(m, p)], axis=0)
            term = jnp.dot(both, table, preferred_element_type=F32)
            term = term + along_x[:, side * HALO + p].reshape(128, 128)
            term = term + local_got[rows, p].reshape(128, 128).astype(F32)
            values.append(term.astype(BF))
            filt_send[rows, p] = values[p].reshape(GROUP, 16, 128)
        for k in ORDER:
            target = ring(k)

            @pl.when(target // GROUP == side)
            def _():
                remote(
                    filt_send.at[target], filtered_ref.at[me], filt_ss.at[k], filt_rs.at[k],
                    at_ring(target),
                ).start()

        value = jnp.concatenate(values, axis=1)
        gram = gram + nt_dot(value, jnp.concatenate([value, psi_lanes(m)], axis=0))

    filtered_ref[me] = filt_send[me]

    even_eight = (lane & 8) == 0
    parts = gram.reshape(GROUP, 2, 8, 256)
    left = jnp.where(even_eight, parts[:, 0, :, :128], parts[:, 1, :, :128])
    right = jnp.where(even_eight, parts[:, 0, :, 128:], parts[:, 1, :, 128:])
    merged = jnp.where(
        even_eight, left + pltpu.roll(left, 120, 2), right + pltpu.roll(right, 8, 2)
    )
    merged = merged.reshape(64, 128)
    for c in range(COLUMNS):
        block = merged[4 * c : 4 * c + 4]
        gram_xy_send[c] = jnp.concatenate([block, jnp.zeros((4, 128), F32)], axis=0)
    gram_xy_got[column] = gram_xy_send[column]
    for k in ORDER:
        to = lax.rem(column + k, COLUMNS)
        copy = remote(
            gram_xy_send.at[to], gram_xy_got.at[column], gxy_ss.at[k], gxy_rs.at[k], at_column(to)
        )
        copy.start()
        sends.append(copy)
    for k in ORDER:
        source = lax.rem(column - k + COLUMNS, COLUMNS)
        slot = gram_xy_got.at[source]
        remote(slot, slot, gxy_ss.at[k], gxy_rs.at[k], at_column(source)).wait_recv()
    rows_x = jnp.sum(gram_xy_got[...], axis=0)
    gram_z_send[...] = rows_x
    gram_z_got[me] = rows_x
    for k in ORDER:
        copy = remote(gram_z_send, gram_z_got.at[me], gz_ss.at[k], gz_rs.at[k], at_ring(ring(k)))
        copy.start()
        sends.append(copy)
    for k in ORDER:
        slot = gram_z_got.at[lax.rem(me - k + RING, RING)]
        remote(gram_z_send, slot, gz_ss.at[k], gz_rs.at[k], at_ring(ring(k))).wait_recv()
    gram_ref[...] = jnp.sum(gram_z_got[...], axis=0) * scale

    for k in ORDER:
        copy = remote(
            filt_send.at[ring(k)], filtered_ref.at[lax.rem(me - k + RING, RING)],
            filt_ss.at[k], filt_rs.at[k], at_ring(ring(k)),
        )
        copy.wait_recv()
        copy.wait_send()
    low_copy(far_got, column + 1).wait_send()
    for copy in sends:
        copy.wait_send()


def shards(orbitals, previous, potential, projectors, strengths, atom_planes):
    band_dev, slab_planes, cells_y, cells_z = orbitals.shape
    space_count, band_count = lax.axis_size("space"), lax.axis_size("band")
    cells = slab_planes * space_count * cells_y * cells_z
    half = lax.rem(lax.axis_index("space"), 2)
    band = lax.axis_index("band")
    vmem = pl.BlockSpec(memory_space=pltpu.VMEM)
    dma = pltpu.SemaphoreType.DMA
    slab_rows = (RING, HALO, 16, 128)
    tile = (8, 128)
    sems = [5, 2] + [RING] * 4 + [2, 2] + [RING] * 12
    filtered, gram = pl.pallas_call(
        lambda *refs: step_kernel(1.0 / cells, *refs),
        out_shape=(
            jax.ShapeDtypeStruct(slab_rows, BF),
            jax.ShapeDtypeStruct(tile, F32),
        ),
        in_specs=[pl.BlockSpec(memory_space=pltpu.HBM)] * 6,
        out_specs=(vmem, vmem),
        scratch_shapes=[
            pltpu.SMEM(atom_planes.shape, jnp.int32),
            pltpu.VMEM(orbitals.shape, F32),
            pltpu.VMEM(orbitals.shape, F32),
            pltpu.VMEM(potential.shape, F32),
            pltpu.VMEM(strengths.shape[::-1], F32),
            pltpu.VMEM((HALO, cells_y, band_dev, cells_z), F32),
            pltpu.VMEM((2, ATOM_DEV, NPJ, BOX, 8, cells_z), BF),
            pltpu.VMEM((ATOM_DEV * ROWS, 128), BF),
            pltpu.VMEM((ATOM_DEV * ROWS, 128), BF),
            pltpu.VMEM((2, 32, 128), BF),
            pltpu.VMEM(slab_rows, BF),
            pltpu.VMEM(slab_rows, BF),
            pltpu.VMEM((4, GROUP, HALO, 16, 128), BF),
            pltpu.VMEM(slab_rows, BF),
            pltpu.VMEM(slab_rows, BF),
            pltpu.VMEM((2, ATOM_DEV, PAD + 2 * BOX, 32, 128), BF),
            pltpu.VMEM((ATOM_DEV, PAD + 2 * BOX, 32, 128), BF),
            pltpu.VMEM((ATOM_DEV * ROWS, 128), BF),
            pltpu.VMEM((ATOM_DEV * ROWS, 128), BF),
            pltpu.VMEM((ATOM_DEV, 192, 128), BF),
            pltpu.VMEM((GROUP, 12, 16, 128), F32),
            pltpu.VMEM((RING,) + tile, F32),
            pltpu.VMEM((RING,) + tile, F32),
            pltpu.VMEM(tile, F32),
            pltpu.VMEM((RING,) + tile, F32),
            pltpu.VMEM((COLUMNS,) + tile, F32),
            pltpu.VMEM((COLUMNS,) + tile, F32),
            pltpu.VMEM(tile, F32),
            pltpu.VMEM((RING,) + tile, F32),
        ]
        + [dma((n,)) for n in sems],
        compiler_params=pltpu.CompilerParams(
            collective_id=0, has_side_effects=True, vmem_limit_bytes=56 << 20
        ),
        name="filter_step",
    )(
        atom_planes,
        orbitals,
        previous,
        potential,
        projectors,
        strengths.T,
    )
    filtered = filtered.reshape(RING, HALO, 2, band_dev, cells_z)
    filtered = filtered.transpose(3, 1, 0, 2, 4).reshape(orbitals.shape)
    gram = gram[:4].reshape(2, 2, GROUP, 2, 8)
    gram = lax.dynamic_index_in_dim(gram, half, 0, keepdims=False)
    gram = lax.dynamic_index_in_dim(gram, band, 1, keepdims=False)
    return filtered, gram[:, 0], gram[:, 1]


def solution(mesh):
    in_specs = (
        P("band", "space", None, None),
        P("band", "space", None, None),
        P("space", None, None),
        P("space", None, None, None, None),
        P(),
        P(),
    )
    out_specs = (P("band", "space", None, None), P("space", "band"), P("space", "band"))
    return jax.shard_map(
        shards, mesh=mesh, in_specs=in_specs, out_specs=out_specs, check_vma=False
    )
```

```python
import jax
import jax.numpy as jnp
from jax import lax
from jax.experimental import pallas as pl
from jax.experimental.pallas import tpu as pltpu
from jax.sharding import PartitionSpec as P

MESH = pl.DeviceIdType.MESH
BF = jnp.bfloat16
F32 = jnp.float32

HALO = 6
BOX = 6
NPJ = 9
ATOM_DEV = 4
RING = 16
GROUP = 8
COLUMNS = 16
SLABS = 32
PAD = BOX - 1
ROWS = 2 * BOX * NPJ
WINDOWS = (0, 96, 208, 304)
CHIP_ORDER = (1, 7, 2, 6, 3, 5, 4)
ORDER = (1, 15, 2, 14, 3, 13, 4, 12, 5, 11, 6, 10, 7, 9, 8)

stencil_weights = (
    -5369.0 / 1800.0,
    12.0 / 7.0,
    -15.0 / 56.0,
    10.0 / 189.0,
    -1.0 / 112.0,
    2.0 / 1925.0,
    -1.0 / 16632.0,
)
center = 5.5
halfwidth = 5.5
gain = 2.0 / halfwidth


def nt_dot(a, b):
    return lax.dot_general(a, b, (((1,), (1,)), ((), ())), preferred_element_type=F32)


def step_kernel(
    scale,
    planes_in,
    psi_in,
    prev_in,
    pot_in,
    proj_ref,
    strength_in,
    filtered_ref,
    gram_ref,
    planes_ref,
    psi_ref,
    prev_ref,
    pot_ref,
    strength_ref,
    psi_rows,
    near,
    own_rows,
    far_rows,
    psi_send,
    local_send,
    window,
    local_got,
    filt_send,
    proj,
    proj_low,
    far_got,
    low_got,
    spread,
    along_x,
    coef_send,
    coef_pair,
    coef_part,
    coef_got,
    coef_all,
    gram_xy_send,
    gram_xy_got,
    gram_z_send,
    gram_z_got,
    load_sem,
    near_sem,
    psi_ss,
    psi_rs,
    halo_ss,
    halo_rs,
    proj_ss,
    proj_rs,
    local_ss,
    local_rs,
    red_ss,
    red_rs,
    all_ss,
    all_rs,
    filt_ss,
    filt_rs,
    gxy_ss,
    gxy_rs,
    gz_ss,
    gz_rs,
):
    space = lax.axis_index("space")
    band = lax.axis_index("band")
    column, half = space // 2, lax.rem(space, 2)
    me = half * GROUP + band

    def ring(k):
        return lax.rem(me + k, RING)

    def at_ring(index):
        return {"space": column * 2 + index // GROUP, "band": lax.rem(index, GROUP)}

    def at_column(col):
        return {"space": lax.rem(col + COLUMNS, COLUMNS) * 2 + half, "band": band}

    def remote(src, dst, ssem, rsem, device):
        return pltpu.make_async_remote_copy(
            src_ref=src, dst_ref=dst, send_sem=ssem, recv_sem=rsem,
            device_id=device, device_id_type=MESH,
        )

    mirror = (1 - half) * GROUP + (3 - band // 2) * 2 + lax.rem(band, 2)

    barrier = pltpu.get_barrier_semaphore()
    peers = [at_ring(ring(k)) for k in ORDER]
    peers += [at_column(column + k) for k in ORDER]
    for peer in peers:
        pl.semaphore_signal(barrier, inc=1, device_id=peer, device_id_type=MESH)

    loads = [
        pltpu.make_async_copy(source, target, load_sem.at[i])
        for i, (source, target) in enumerate(
            (
                (psi_in, psi_ref),
                (strength_in, strength_ref),
                (planes_in, planes_ref),
                (pot_in, pot_ref),
                (prev_in, prev_ref),
            )
        )
    ]
    fetches = {}
    for i, pair in ((1, mirror), (0, me)):
        block = pl.ds(pl.multiple_of(pair // 4 * 8, 8), 8)
        fetch = pltpu.make_async_copy(proj_ref.at[:, :, :, block, :], near.at[i], near_sem.at[i])
        fetch.start()
        fetches[i] = fetch
        if i:
            loads[0].start()
    for load in loads[1:]:
        load.start()

    pick_row = lax.broadcasted_iota(jnp.int32, (32, 128), 0)
    pick_from = lax.broadcasted_iota(jnp.int32, (32, 128), 1)

    def pick_rows(i, pair, rows_ref):
        wanted = 8 * (pick_row >> 1) + 2 * lax.rem(pair, 4) + (pick_row & 1)
        pick = jnp.where(pick_from == wanted, 1.0, 0.0).astype(BF)
        fetches[i].wait()
        flat = near[i].reshape(ATOM_DEV * ROWS * 4, 128)
        for g in range(14):
            first = min(128 * g, ATOM_DEV * ROWS * 4 - 128)
            rows = jnp.dot(pick, flat[first : first + 128], preferred_element_type=F32)
            rows_ref[first // 4 : first // 4 + 32] = rows.astype(BF)

    pick_rows(1, mirror, far_rows)

    loads[0].wait()

    def pack(p, carry):
        turned = jnp.swapaxes(psi_ref[:, p], 0, 1)
        psi_rows[p] = turned
        psi_send[:, p] = turned.reshape(RING, 16, 128).astype(BF)
        return carry

    lax.fori_loop(0, HALO, pack, 0)
    window[1 + half, band] = psi_send[me]

    pl.semaphore_wait(barrier, len(peers))

    sends = []
    far_copy = remote(far_rows, far_got, proj_ss.at[0], proj_rs.at[0], at_ring(mirror))

    def low_copy(rows_ref, col):
        return remote(rows_ref, low_got, proj_ss.at[1], proj_rs.at[1], at_column(col))

    for k in ORDER:
        copy = remote(
            psi_send.at[ring(k)], window.at[1 + half, band], psi_ss.at[k], psi_rs.at[k],
            at_ring(ring(k)),
        )
        copy.start()
        sends.append(copy)

    far_copy.start()
    sends.append(far_copy)
    pick_rows(0, me, own_rows)

    @pl.when(half == 1)
    def _():
        low_copy(own_rows, column + 1).start()

    for k in range(3):
        table = proj.at[k - 1] if k else proj_low
        table[:, 0:PAD] = jnp.zeros((ATOM_DEV, PAD, 32, 128), BF)
        table[:, PAD + BOX :] = jnp.zeros((ATOM_DEV, BOX, 32, 128), BF)

    row = lax.broadcasted_iota(jnp.int32, (192, 128), 0)
    source_row = lax.broadcasted_iota(jnp.int32, (192, 128), 1) - 12 * (row & 15) - (row >> 4)
    for a in range(ATOM_DEV):
        hit = (source_row == ROWS * a - WINDOWS[a]) & ((row & 15) < NPJ)
        spread[a] = jnp.where(hit, 1.0, 0.0).astype(BF)

    def expand(rows_ref, table):
        for a in range(ATOM_DEV):
            rows = rows_ref[WINDOWS[a] : WINDOWS[a] + 128]
            moved = jnp.dot(spread[a], rows, preferred_element_type=F32)
            table[a, PAD : PAD + BOX] = moved.astype(BF).reshape(BOX, 32, 128)

    expand(own_rows, proj.at[half])

    loads[1].wait()
    loads[2].wait()
    lane_row = lax.broadcasted_iota(jnp.int32, (128, 128), 0)
    lane_col = lax.broadcasted_iota(jnp.int32, (128, 128), 1)
    own_lane = lax.broadcasted_iota(jnp.int32, (NPJ, 128), 0)
    own_lane = own_lane == (lax.broadcasted_iota(jnp.int32, (NPJ, 128), 1) & 15)
    slabs = [lax.rem(2 * column - 1 + k + SLABS, SLABS) for k in range(3)]
    levels = []
    for k in range(3):
        take = jnp.where(lane_row == slabs[k] * ATOM_DEV + (lane_col >> 5), 1.0, 0.0)
        spread_levels = jnp.dot(
            strength_ref[...], take, precision=lax.Precision.HIGHEST, preferred_element_type=F32
        )
        picked = jnp.where(own_lane, spread_levels, 0.0)
        levels.append(gain * jnp.sum(picked, axis=0, keepdims=True))

    loads[3].wait()
    loads[4].wait()
    def local_terms(p, carry):
        field = psi_rows[p]
        flat = field.reshape(256, 128)
        total = (3.0 * stencil_weights[0]) * field
        for m in range(1, HALO + 1):
            ahead = jnp.concatenate([field[m:], field[:m]], axis=0)
            behind = jnp.concatenate([field[32 - m :], field[: 32 - m]], axis=0)
            turned = pltpu.roll(flat, m, 1) + pltpu.roll(flat, 128 - m, 1)
            total = total + stencil_weights[m] * (ahead + behind + turned.reshape(32, 8, 128))
        level = pot_ref[p][:, None, :] - center
        local = gain * (level * field - 0.5 * total) - jnp.swapaxes(prev_ref[:, p], 0, 1)
        local_send[:, p] = local.reshape(RING, 16, 128).astype(BF)
        return carry

    lax.fori_loop(0, HALO, local_terms, 0)
    local_got[me] = local_send[me]

    for k in ORDER:
        copy = remote(
            local_send.at[ring(k)], local_got.at[me], local_ss.at[k], local_rs.at[k],
            at_ring(ring(k)),
        )
        copy.start()
        sends.append(copy)

    far_copy.wait_recv()

    @pl.when(half == 0)
    def _():
        low_copy(far_got, column + 1).start()

    for k in (0,) + ORDER:
        source = lax.rem(me - k + RING, RING)
        side, group = source // GROUP, lax.rem(source, GROUP)
        piece = window.at[1 + side, group]
        if k:
            remote(piece, piece, psi_ss.at[k], psi_rs.at[k], at_ring(source)).wait_recv()
        copy = remote(
            piece, window.at[3 - 3 * side, group], halo_ss.at[k], halo_rs.at[k],
            at_column(column + 2 * side - 1),
        )
        copy.start()
        sends.append(copy)

    def start(k, a):
        return jnp.clip(planes_ref[slabs[k] * ATOM_DEV + a] - slabs[k] * HALO, 0, HALO - 1)

    starts = [[start(k, a) for a in range(ATOM_DEV)] for k in range(3)]

    def stack(k, plane):
        table = proj.at[k - 1] if k else proj_low
        rows = [table[a, plane - starts[k][a] + PAD] for a in range(ATOM_DEV)]
        return jnp.concatenate(rows, axis=0)

    def psi_plane(m, p):
        return window[m, :, p].reshape(128, 128)

    def psi_lanes(m):
        return jnp.concatenate([psi_plane(m, p) for p in range(HALO)], axis=1)

    def stack_lanes(k, first):
        return jnp.concatenate([stack(k, first + p) for p in range(HALO)], axis=1)

    expand(far_got, proj.at[1 - half])
    coef_mid = nt_dot(psi_lanes(1), stack_lanes(1, 0)) + nt_dot(psi_lanes(2), stack_lanes(1, HALO))
    coef_high = nt_dot(psi_lanes(2), stack_lanes(2, 0))
    low_copy(far_got, column - 1).wait_recv()
    expand(low_got, proj_low)
    coef_low = nt_dot(psi_lanes(1), stack_lanes(0, HALO))
    for k in (0,) + ORDER:
        source = lax.rem(me - k + RING, RING)
        side, group = source // GROUP, lax.rem(source, GROUP)
        slot = window.at[3 - 3 * side, group]
        remote(
            slot, slot, halo_ss.at[k], halo_rs.at[k], at_column(column + 2 * side - 1)
        ).wait_recv()
    coef_low = coef_low + nt_dot(psi_lanes(0), stack_lanes(0, 0))
    coef_high = coef_high + nt_dot(psi_lanes(3), stack_lanes(2, HALO))

    lane = lax.broadcasted_iota(jnp.int32, (GROUP, 8, 128), 2)
    even_row = (lane & 16) == 0

    def swap(value):
        up = pltpu.roll(value, 16, 2)
        down = pltpu.roll(value, 112, 2)
        return jnp.where(even_row, down, up)

    folded = []
    for coef in (coef_low, coef_mid, coef_high):
        parts = coef.reshape(GROUP, 2, 8, 128)
        mixed = jnp.where(even_row, parts[:, 0], parts[:, 1])
        folded.append(mixed + swap(mixed))
    coef_send[0:GROUP] = jnp.where(even_row, folded[0], folded[1])
    coef_send[GROUP:] = folded[2]

    core = lax.rem(band, 2)
    chip = me // 2
    sibling = {"band": band + 1 - 2 * core}
    kept, given = pl.ds(core * GROUP, GROUP), pl.ds((1 - core) * GROUP, GROUP)
    copy = remote(coef_send.at[given], coef_pair, red_ss.at[0], red_rs.at[0], sibling)
    copy.start()
    sends.append(copy)
    copy.wait_recv()
    coef_part[...] = (coef_send[kept] + coef_pair[...]).reshape(4, 16, 128).astype(BF)
    coef_got[chip] = coef_part[...]
    for k in CHIP_ORDER:
        copy = remote(
            coef_part, coef_got.at[chip], all_ss.at[k], all_rs.at[k], at_ring(ring(2 * k))
        )
        copy.start()
        sends.append(copy)

    def stencil_x(group, carry):
        planes = window[:, group].reshape(24, 16, 128).astype(F32)
        total = jnp.zeros((12, 16, 128), F32)
        for m in range(1, HALO + 1):
            pair = planes[HALO - m : 18 - m] + planes[HALO + m : 18 + m]
            total = total + (-0.5 * gain * stencil_weights[m]) * pair
        along_x[group] = total
        return carry

    lax.fori_loop(0, GROUP, stencil_x, 0)

    for k in CHIP_ORDER:
        slot = coef_got.at[lax.rem(chip - k + 8, 8)]
        remote(slot, slot, all_ss.at[k], all_rs.at[k], at_ring(ring(2 * k))).wait_recv()
    coef_all[kept] = jnp.sum(coef_got[...].astype(F32), axis=0).reshape(GROUP, 8, 128)
    copy = remote(coef_all.at[kept], coef_all.at[kept], red_ss.at[1], red_rs.at[1], sibling)
    copy.start()
    sends.append(copy)
    remote(coef_all.at[given], coef_all.at[given], red_ss.at[1], red_rs.at[1], sibling).wait_recv()

    shared = coef_all[0:GROUP]
    crossed = swap(shared)
    full = [
        jnp.where(even_row, shared, crossed),
        jnp.where(even_row, crossed, shared),
        coef_all[GROUP:],
    ]
    weights = []
    for k in range(3):
        weighted = full[k] * levels[k]
        rows = [jnp.where(even_row, weighted, 0.0), jnp.where(even_row, 0.0, weighted)]
        weights.append(jnp.stack(rows, axis=1).reshape(128, 128).astype(BF))

    for k in ORDER:
        slot = local_got.at[lax.rem(me - k + RING, RING)]
        remote(slot, slot, local_ss.at[k], local_rs.at[k], at_ring(ring(k))).wait_recv()

    gram = jnp.zeros((128, 256), F32)
    for m in (1, 2):
        side = m - 1
        both = jnp.concatenate([weights[m - 1], weights[m]], axis=1)
        rows = pl.ds(side * GROUP, GROUP)

        values = []
        for p in range(HALO):
            table = jnp.concatenate([stack(m - 1, HALO + p), stack(m, p)], axis=0)
            term = jnp.dot(both, table, preferred_element_type=F32)
            term = term + along_x[:, side * HALO + p].reshape(128, 128)
            term = term + local_got[rows, p].reshape(128, 128).astype(F32)
            values.append(term.astype(BF))
            filt_send[rows, p] = values[p].reshape(GROUP, 16, 128)
        for k in ORDER:
            target = ring(k)

            @pl.when(target // GROUP == side)
            def _():
                remote(
                    filt_send.at[target], filtered_ref.at[me], filt_ss.at[k], filt_rs.at[k],
                    at_ring(target),
                ).start()

        value = jnp.concatenate(values, axis=1)
        gram = gram + nt_dot(value, jnp.concatenate([value, psi_lanes(m)], axis=0))

    filtered_ref[me] = filt_send[me]

    even_eight = (lane & 8) == 0
    parts = gram.reshape(GROUP, 2, 8, 256)
    left = jnp.where(even_eight, parts[:, 0, :, :128], parts[:, 1, :, :128])
    right = jnp.where(even_eight, parts[:, 0, :, 128:], parts[:, 1, :, 128:])
    merged = jnp.where(
        even_eight, left + pltpu.roll(left, 120, 2), right + pltpu.roll(right, 8, 2)
    )
    merged = merged.reshape(64, 128)
    for c in range(COLUMNS):
        block = merged[4 * c : 4 * c + 4]
        gram_xy_send[c] = jnp.concatenate([block, jnp.zeros((4, 128), F32)], axis=0)
    gram_xy_got[column] = gram_xy_send[column]
    for k in ORDER:
        to = lax.rem(column + k, COLUMNS)
        copy = remote(
            gram_xy_send.at[to], gram_xy_got.at[column], gxy_ss.at[k], gxy_rs.at[k], at_column(to)
        )
        copy.start()
        sends.append(copy)
    for k in ORDER:
        source = lax.rem(column - k + COLUMNS, COLUMNS)
        slot = gram_xy_got.at[source]
        remote(slot, slot, gxy_ss.at[k], gxy_rs.at[k], at_column(source)).wait_recv()
    rows_x = jnp.sum(gram_xy_got[...], axis=0)
    gram_z_send[...] = rows_x
    gram_z_got[me] = rows_x
    for k in ORDER:
        copy = remote(gram_z_send, gram_z_got.at[me], gz_ss.at[k], gz_rs.at[k], at_ring(ring(k)))
        copy.start()
        sends.append(copy)
    for k in ORDER:
        slot = gram_z_got.at[lax.rem(me - k + RING, RING)]
        remote(gram_z_send, slot, gz_ss.at[k], gz_rs.at[k], at_ring(ring(k))).wait_recv()
    gram_ref[...] = jnp.sum(gram_z_got[...], axis=0) * scale

    for k in ORDER:
        copy = remote(
            filt_send.at[ring(k)], filtered_ref.at[lax.rem(me - k + RING, RING)],
            filt_ss.at[k], filt_rs.at[k], at_ring(ring(k)),
        )
        copy.wait_recv()
        copy.wait_send()
    low_copy(far_got, column + 1).wait_send()
    for copy in sends:
        copy.wait_send()


def shards(orbitals, previous, potential, projectors, strengths, atom_planes):
    band_dev, slab_planes, cells_y, cells_z = orbitals.shape
    space_count, band_count = lax.axis_size("space"), lax.axis_size("band")
    cells = slab_planes * space_count * cells_y * cells_z
    half = lax.rem(lax.axis_index("space"), 2)
    band = lax.axis_index("band")
    vmem = pl.BlockSpec(memory_space=pltpu.VMEM)
    dma = pltpu.SemaphoreType.DMA
    slab_rows = (RING, HALO, 16, 128)
    tile = (8, 128)
    sems = [5, 2] + [RING] * 4 + [2, 2] + [RING] * 12
    filtered, gram = pl.pallas_call(
        lambda *refs: step_kernel(1.0 / cells, *refs),
        out_shape=(
            jax.ShapeDtypeStruct(slab_rows, BF),
            jax.ShapeDtypeStruct(tile, F32),
        ),
        in_specs=[pl.BlockSpec(memory_space=pltpu.HBM)] * 6,
        out_specs=(vmem, vmem),
        scratch_shapes=[
            pltpu.SMEM(atom_planes.shape, jnp.int32),
            pltpu.VMEM(orbitals.shape, F32),
            pltpu.VMEM(orbitals.shape, F32),
            pltpu.VMEM(potential.shape, F32),
            pltpu.VMEM(strengths.shape[::-1], F32),
            pltpu.VMEM((HALO, cells_y, band_dev, cells_z), F32),
            pltpu.VMEM((2, ATOM_DEV, NPJ, BOX, 8, cells_z), BF),
            pltpu.VMEM((ATOM_DEV * ROWS, 128), BF),
            pltpu.VMEM((ATOM_DEV * ROWS, 128), BF),
            pltpu.VMEM(slab_rows, BF),
            pltpu.VMEM(slab_rows, BF),
            pltpu.VMEM((4, GROUP, HALO, 16, 128), BF),
            pltpu.VMEM(slab_rows, BF),
            pltpu.VMEM(slab_rows, BF),
            pltpu.VMEM((2, ATOM_DEV, PAD + 2 * BOX, 32, 128), BF),
            pltpu.VMEM((ATOM_DEV, PAD + 2 * BOX, 32, 128), BF),
            pltpu.VMEM((ATOM_DEV * ROWS, 128), BF),
            pltpu.VMEM((ATOM_DEV * ROWS, 128), BF),
            pltpu.VMEM((ATOM_DEV, 192, 128), BF),
            pltpu.VMEM((GROUP, 12, 16, 128), F32),
            pltpu.VMEM((RING,) + tile, F32),
            pltpu.VMEM((GROUP,) + tile, F32),
            pltpu.VMEM((4, 16, 128), BF),
            pltpu.VMEM((8, 4, 16, 128), BF),
            pltpu.VMEM((RING,) + tile, F32),
            pltpu.VMEM((COLUMNS,) + tile, F32),
            pltpu.VMEM((COLUMNS,) + tile, F32),
            pltpu.VMEM(tile, F32),
            pltpu.VMEM((RING,) + tile, F32),
        ]
        + [dma((n,)) for n in sems],
        compiler_params=pltpu.CompilerParams(
            collective_id=0, has_side_effects=True, vmem_limit_bytes=50 << 20
        ),
        name="filter_step",
    )(
        *(
            pltpu.with_memory_space_constraint(operand, pltpu.HBM)
            for operand in (
                atom_planes, orbitals, previous, potential, projectors, strengths.T
            )
        )
    )
    filtered = filtered.reshape(RING, HALO, 2, band_dev, cells_z)
    filtered = filtered.transpose(3, 1, 0, 2, 4).reshape(orbitals.shape)
    gram = gram[:4].reshape(2, 2, GROUP, 2, 8)
    gram = lax.dynamic_index_in_dim(gram, half, 0, keepdims=False)
    gram = lax.dynamic_index_in_dim(gram, band, 1, keepdims=False)
    return filtered, gram[:, 0], gram[:, 1]


def solution(mesh):
    in_specs = (
        P("band", "space", None, None),
        P("band", "space", None, None),
        P("space", None, None),
        P("space", None, None, None, None),
        P(),
        P(),
    )
    out_specs = (P("band", "space", None, None), P("space", "band"), P("space", "band"))
    return jax.shard_map(
        shards, mesh=mesh, in_specs=in_specs, out_specs=out_specs, check_vma=False
    )
```

```python
import jax
import jax.numpy as jnp
from jax import lax
from jax.experimental import pallas as pl
from jax.experimental.pallas import tpu as pltpu
from jax.sharding import PartitionSpec as P

MESH = pl.DeviceIdType.MESH
BF = jnp.bfloat16
F32 = jnp.float32

HALO = 6
BOX = 6
NPJ = 9
ATOM_DEV = 4
RING = 16
GROUP = 8
COLUMNS = 16
SLABS = 32
PAD = BOX - 1
ROWS = 2 * BOX * NPJ
WINDOWS = (0, 96, 208, 304)
CHIP_ORDER = (4, 3, 5, 2, 6, 1, 7)
ORDER = (8, 9, 7, 6, 10, 5, 11, 4, 12, 3, 13, 2, 14, 1, 15)

stencil_weights = (
    -5369.0 / 1800.0,
    12.0 / 7.0,
    -15.0 / 56.0,
    10.0 / 189.0,
    -1.0 / 112.0,
    2.0 / 1925.0,
    -1.0 / 16632.0,
)
center = 5.5
halfwidth = 5.5
gain = 2.0 / halfwidth


def nt_dot(a, b):
    return lax.dot_general(a, b, (((1,), (1,)), ((), ())), preferred_element_type=F32)


def step_kernel(
    scale,
    planes_in,
    psi_in,
    prev_in,
    pot_in,
    proj_ref,
    strength_in,
    filtered_ref,
    gram_ref,
    planes_ref,
    psi_ref,
    prev_ref,
    pot_ref,
    strength_ref,
    psi_rows,
    near,
    own_rows,
    far_rows,
    psi_send,
    local_send,
    window,
    local_got,
    filt_send,
    proj,
    proj_low,
    far_got,
    low_got,
    spread,
    along_x,
    coef_send,
    coef_pair,
    coef_part,
    coef_got,
    coef_all,
    gram_xy_send,
    gram_xy_got,
    gram_z_send,
    gram_z_got,
    load_sem,
    near_sem,
    psi_ss,
    psi_rs,
    halo_ss,
    halo_rs,
    proj_ss,
    proj_rs,
    local_ss,
    local_rs,
    red_ss,
    red_rs,
    all_ss,
    all_rs,
    filt_ss,
    filt_rs,
    gxy_ss,
    gxy_rs,
    gz_ss,
    gz_rs,
):
    space = lax.axis_index("space")
    band = lax.axis_index("band")
    column, half = space // 2, lax.rem(space, 2)
    me = half * GROUP + band

    def ring(k):
        return lax.rem(me + k, RING)

    def at_ring(index):
        return {"space": column * 2 + index // GROUP, "band": lax.rem(index, GROUP)}

    def at_column(col):
        return {"space": lax.rem(col + COLUMNS, COLUMNS) * 2 + half, "band": band}

    def remote(src, dst, ssem, rsem, device):
        return pltpu.make_async_remote_copy(
            src_ref=src, dst_ref=dst, send_sem=ssem, recv_sem=rsem,
            device_id=device, device_id_type=MESH,
        )

    mirror = (1 - half) * GROUP + (3 - band // 2) * 2 + lax.rem(band, 2)

    barrier = pltpu.get_barrier_semaphore()
    peers = [at_ring(ring(k)) for k in ORDER]
    peers += [at_column(column + k) for k in ORDER]
    for peer in peers:
        pl.semaphore_signal(barrier, inc=1, device_id=peer, device_id_type=MESH)

    loads = [
        pltpu.make_async_copy(source, target, load_sem.at[i])
        for i, (source, target) in enumerate(
            (
                (psi_in, psi_ref),
                (strength_in, strength_ref),
                (planes_in, planes_ref),
                (pot_in, pot_ref),
                (prev_in, prev_ref),
            )
        )
    ]
    fetches = {}
    for i, pair in ((1, mirror), (0, me)):
        block = pl.ds(pl.multiple_of(pair // 4 * 8, 8), 8)
        fetch = pltpu.make_async_copy(proj_ref.at[:, :, :, block, :], near.at[i], near_sem.at[i])
        fetch.start()
        fetches[i] = fetch
        if i:
            loads[0].start()
    for load in loads[1:]:
        load.start()

    pick_row = lax.broadcasted_iota(jnp.int32, (32, 128), 0)
    pick_from = lax.broadcasted_iota(jnp.int32, (32, 128), 1)

    def pick_rows(i, pair, rows_ref):
        wanted = 8 * (pick_row >> 1) + 2 * lax.rem(pair, 4) + (pick_row & 1)
        pick = jnp.where(pick_from == wanted, 1.0, 0.0).astype(BF)
        fetches[i].wait()
        flat = near[i].reshape(ATOM_DEV * ROWS * 4, 128)
        for g in range(14):
            first = min(128 * g, ATOM_DEV * ROWS * 4 - 128)
            rows = jnp.dot(pick, flat[first : first + 128], preferred_element_type=F32)
            rows_ref[first // 4 : first // 4 + 32] = rows.astype(BF)

    pick_rows(1, mirror, far_rows)

    loads[0].wait()

    def pack(p, carry):
        turned = jnp.swapaxes(psi_ref[:, p], 0, 1)
        psi_rows[p] = turned
        psi_send[:, p] = turned.reshape(RING, 16, 128).astype(BF)
        return carry

    lax.fori_loop(0, HALO, pack, 0)
    window[1 + half, band] = psi_send[me]

    pl.semaphore_wait(barrier, len(peers))

    sends = []
    far_copy = remote(far_rows, far_got, proj_ss.at[0], proj_rs.at[0], at_ring(mirror))

    def low_copy(rows_ref, col):
        return remote(rows_ref, low_got, proj_ss.at[1], proj_rs.at[1], at_column(col))

    far_copy.start()
    sends.append(far_copy)
    pick_rows(0, me, own_rows)

    @pl.when(half == 1)
    def _():
        low_copy(own_rows, column + 1).start()

    for k in ORDER:
        copy = remote(
            psi_send.at[ring(k)], window.at[1 + half, band], psi_ss.at[k], psi_rs.at[k],
            at_ring(ring(k)),
        )
        copy.start()
        sends.append(copy)

    for k in range(3):
        table = proj.at[k - 1] if k else proj_low
        table[:, 0:PAD] = jnp.zeros((ATOM_DEV, PAD, 32, 128), BF)
        table[:, PAD + BOX :] = jnp.zeros((ATOM_DEV, BOX, 32, 128), BF)

    row = lax.broadcasted_iota(jnp.int32, (192, 128), 0)
    source_row = lax.broadcasted_iota(jnp.int32, (192, 128), 1) - 12 * (row & 15) - (row >> 4)
    for a in range(ATOM_DEV):
        hit = (source_row == ROWS * a - WINDOWS[a]) & ((row & 15) < NPJ)
        spread[a] = jnp.where(hit, 1.0, 0.0).astype(BF)

    def expand(rows_ref, table):
        for a in range(ATOM_DEV):
            rows = rows_ref[WINDOWS[a] : WINDOWS[a] + 128]
            moved = jnp.dot(spread[a], rows, preferred_element_type=F32)
            table[a, PAD : PAD + BOX] = moved.astype(BF).reshape(BOX, 32, 128)

    expand(own_rows, proj.at[half])

    loads[1].wait()
    loads[2].wait()
    lane_row = lax.broadcasted_iota(jnp.int32, (128, 128), 0)
    lane_col = lax.broadcasted_iota(jnp.int32, (128, 128), 1)
    own_lane = lax.broadcasted_iota(jnp.int32, (NPJ, 128), 0)
    own_lane = own_lane == (lax.broadcasted_iota(jnp.int32, (NPJ, 128), 1) & 15)
    slabs = [lax.rem(2 * column - 1 + k + SLABS, SLABS) for k in range(3)]
    levels = []
    for k in range(3):
        take = jnp.where(lane_row == slabs[k] * ATOM_DEV + (lane_col >> 5), 1.0, 0.0)
        spread_levels = jnp.dot(
            strength_ref[...], take, precision=lax.Precision.HIGHEST, preferred_element_type=F32
        )
        picked = jnp.where(own_lane, spread_levels, 0.0)
        levels.append(gain * jnp.sum(picked, axis=0, keepdims=True))

    loads[3].wait()
    loads[4].wait()
    def local_terms(p, carry):
        field = psi_rows[p]
        flat = field.reshape(256, 128)
        total = (3.0 * stencil_weights[0]) * field
        for m in range(1, HALO + 1):
            ahead = jnp.concatenate([field[m:], field[:m]], axis=0)
            behind = jnp.concatenate([field[32 - m :], field[: 32 - m]], axis=0)
            turned = pltpu.roll(flat, m, 1) + pltpu.roll(flat, 128 - m, 1)
            total = total + stencil_weights[m] * (ahead + behind + turned.reshape(32, 8, 128))
        level = pot_ref[p][:, None, :] - center
        local = gain * (level * field - 0.5 * total) - jnp.swapaxes(prev_ref[:, p], 0, 1)
        local_send[:, p] = local.reshape(RING, 16, 128).astype(BF)
        return carry

    lax.fori_loop(0, HALO, local_terms, 0)
    local_got[me] = local_send[me]

    for k in ORDER:
        copy = remote(
            local_send.at[ring(k)], local_got.at[me], local_ss.at[k], local_rs.at[k],
            at_ring(ring(k)),
        )
        copy.start()
        sends.append(copy)

    far_copy.wait_recv()

    @pl.when(half == 0)
    def _():
        low_copy(far_got, column + 1).start()

    for k in (0,) + ORDER:
        source = lax.rem(me - k + RING, RING)
        side, group = source // GROUP, lax.rem(source, GROUP)
        piece = window.at[1 + side, group]
        if k:
            remote(piece, piece, psi_ss.at[k], psi_rs.at[k], at_ring(source)).wait_recv()
        copy = remote(
            piece, window.at[3 - 3 * side, group], halo_ss.at[k], halo_rs.at[k],
            at_column(column + 2 * side - 1),
        )
        copy.start()
        sends.append(copy)

    def start(k, a):
        return jnp.clip(planes_ref[slabs[k] * ATOM_DEV + a] - slabs[k] * HALO, 0, HALO - 1)

    starts = [[start(k, a) for a in range(ATOM_DEV)] for k in range(3)]

    def stack(k, plane):
        table = proj.at[k - 1] if k else proj_low
        rows = [table[a, plane - starts[k][a] + PAD] for a in range(ATOM_DEV)]
        return jnp.concatenate(rows, axis=0)

    def psi_plane(m, p):
        return window[m, :, p].reshape(128, 128)

    def psi_lanes(m):
        return jnp.concatenate([psi_plane(m, p) for p in range(HALO)], axis=1)

    def stack_lanes(k, first):
        return jnp.concatenate([stack(k, first + p) for p in range(HALO)], axis=1)

    expand(far_got, proj.at[1 - half])
    coef_mid = nt_dot(psi_lanes(1), stack_lanes(1, 0)) + nt_dot(psi_lanes(2), stack_lanes(1, HALO))
    coef_high = nt_dot(psi_lanes(2), stack_lanes(2, 0))
    low_copy(far_got, column - 1).wait_recv()
    expand(low_got, proj_low)
    coef_low = nt_dot(psi_lanes(1), stack_lanes(0, HALO))
    for k in (0,) + ORDER:
        source = lax.rem(me - k + RING, RING)
        side, group = source // GROUP, lax.rem(source, GROUP)
        slot = window.at[3 - 3 * side, group]
        remote(
            slot, slot, halo_ss.at[k], halo_rs.at[k], at_column(column + 2 * side - 1)
        ).wait_recv()
    coef_low = coef_low + nt_dot(psi_lanes(0), stack_lanes(0, 0))
    coef_high = coef_high + nt_dot(psi_lanes(3), stack_lanes(2, HALO))

    lane = lax.broadcasted_iota(jnp.int32, (GROUP, 8, 128), 2)
    even_row = (lane & 16) == 0

    def swap(value):
        up = pltpu.roll(value, 16, 2)
        down = pltpu.roll(value, 112, 2)
        return jnp.where(even_row, down, up)

    folded = []
    for coef in (coef_low, coef_mid, coef_high):
        parts = coef.reshape(GROUP, 2, 8, 128)
        mixed = jnp.where(even_row, parts[:, 0], parts[:, 1])
        folded.append(mixed + swap(mixed))
    coef_send[0:GROUP] = jnp.where(even_row, folded[0], folded[1])
    coef_send[GROUP:] = folded[2]

    core = lax.rem(band, 2)
    chip = me // 2
    sibling = {"band": band + 1 - 2 * core}
    kept, given = pl.ds(core * GROUP, GROUP), pl.ds((1 - core) * GROUP, GROUP)
    copy = remote(coef_send.at[given], coef_pair, red_ss.at[0], red_rs.at[0], sibling)
    copy.start()
    sends.append(copy)
    copy.wait_recv()
    coef_part[...] = (coef_send[kept] + coef_pair[...]).reshape(4, 16, 128).astype(BF)
    coef_got[chip] = coef_part[...]
    for k in CHIP_ORDER:
        copy = remote(
            coef_part, coef_got.at[chip], all_ss.at[k], all_rs.at[k], at_ring(ring(2 * k))
        )
        copy.start()
        sends.append(copy)

    def stencil_x(group, carry):
        planes = window[:, group].reshape(24, 16, 128).astype(F32)
        total = jnp.zeros((12, 16, 128), F32)
        for m in range(1, HALO + 1):
            pair = planes[HALO - m : 18 - m] + planes[HALO + m : 18 + m]
            total = total + (-0.5 * gain * stencil_weights[m]) * pair
        along_x[group] = total
        return carry

    lax.fori_loop(0, GROUP, stencil_x, 0)

    for k in CHIP_ORDER:
        slot = coef_got.at[lax.rem(chip - k + 8, 8)]
        remote(slot, slot, all_ss.at[k], all_rs.at[k], at_ring(ring(2 * k))).wait_recv()
    coef_all[kept] = jnp.sum(coef_got[...].astype(F32), axis=0).reshape(GROUP, 8, 128)
    copy = remote(coef_all.at[kept], coef_all.at[kept], red_ss.at[1], red_rs.at[1], sibling)
    copy.start()
    sends.append(copy)
    remote(coef_all.at[given], coef_all.at[given], red_ss.at[1], red_rs.at[1], sibling).wait_recv()

    shared = coef_all[0:GROUP]
    crossed = swap(shared)
    full = [
        jnp.where(even_row, shared, crossed),
        jnp.where(even_row, crossed, shared),
        coef_all[GROUP:],
    ]
    weights = []
    for k in range(3):
        weighted = full[k] * levels[k]
        rows = [jnp.where(even_row, weighted, 0.0), jnp.where(even_row, 0.0, weighted)]
        weights.append(jnp.stack(rows, axis=1).reshape(128, 128).astype(BF))

    for k in ORDER:
        slot = local_got.at[lax.rem(me - k + RING, RING)]
        remote(slot, slot, local_ss.at[k], local_rs.at[k], at_ring(ring(k))).wait_recv()

    gram = jnp.zeros((128, 256), F32)
    for m in (1, 2):
        side = m - 1
        both = jnp.concatenate([weights[m - 1], weights[m]], axis=1)
        rows = pl.ds(side * GROUP, GROUP)

        values = []
        for p in range(HALO):
            table = jnp.concatenate([stack(m - 1, HALO + p), stack(m, p)], axis=0)
            term = jnp.dot(both, table, preferred_element_type=F32)
            term = term + along_x[:, side * HALO + p].reshape(128, 128)
            term = term + local_got[rows, p].reshape(128, 128).astype(F32)
            values.append(term.astype(BF))
            filt_send[rows, p] = values[p].reshape(GROUP, 16, 128)
        for k in ORDER:
            target = ring(k)

            @pl.when(target // GROUP == side)
            def _():
                remote(
                    filt_send.at[target], filtered_ref.at[me], filt_ss.at[k], filt_rs.at[k],
                    at_ring(target),
                ).start()

        value = jnp.concatenate(values, axis=1)
        gram = gram + nt_dot(value, jnp.concatenate([value, psi_lanes(m)], axis=0))

    filtered_ref[me] = filt_send[me]

    even_eight = (lane & 8) == 0
    parts = gram.reshape(GROUP, 2, 8, 256)
    left = jnp.where(even_eight, parts[:, 0, :, :128], parts[:, 1, :, :128])
    right = jnp.where(even_eight, parts[:, 0, :, 128:], parts[:, 1, :, 128:])
    merged = jnp.where(
        even_eight, left + pltpu.roll(left, 120, 2), right + pltpu.roll(right, 8, 2)
    )
    merged = merged.reshape(64, 128)
    for c in range(COLUMNS):
        block = merged[4 * c : 4 * c + 4]
        gram_xy_send[c] = jnp.concatenate([block, jnp.zeros((4, 128), F32)], axis=0)
    gram_xy_got[column] = gram_xy_send[column]
    for k in ORDER:
        to = lax.rem(column + k, COLUMNS)
        copy = remote(
            gram_xy_send.at[to], gram_xy_got.at[column], gxy_ss.at[k], gxy_rs.at[k], at_column(to)
        )
        copy.start()
        sends.append(copy)
    for k in ORDER:
        source = lax.rem(column - k + COLUMNS, COLUMNS)
        slot = gram_xy_got.at[source]
        remote(slot, slot, gxy_ss.at[k], gxy_rs.at[k], at_column(source)).wait_recv()
    rows_x = jnp.sum(gram_xy_got[...], axis=0)
    gram_z_send[...] = rows_x
    gram_z_got[me] = rows_x
    for k in ORDER:
        copy = remote(gram_z_send, gram_z_got.at[me], gz_ss.at[k], gz_rs.at[k], at_ring(ring(k)))
        copy.start()
        sends.append(copy)
    for k in ORDER:
        slot = gram_z_got.at[lax.rem(me - k + RING, RING)]
        remote(gram_z_send, slot, gz_ss.at[k], gz_rs.at[k], at_ring(ring(k))).wait_recv()
    total = jnp.sum(gram_z_got[...], axis=0) * scale
    total = pltpu.roll(total, lax.rem(128 - 16 * band, 128), 1)
    gram_ref[...] = jnp.where(half == 0, total, pltpu.roll(total, 6, 0))

    for k in ORDER:
        copy = remote(
            filt_send.at[ring(k)], filtered_ref.at[lax.rem(me - k + RING, RING)],
            filt_ss.at[k], filt_rs.at[k], at_ring(ring(k)),
        )
        copy.wait_recv()
        copy.wait_send()
    low_copy(far_got, column + 1).wait_send()
    for copy in sends:
        copy.wait_send()


def shards(orbitals, previous, potential, projectors, strengths, atom_planes):
    band_dev, slab_planes, cells_y, cells_z = orbitals.shape
    space_count, band_count = lax.axis_size("space"), lax.axis_size("band")
    cells = slab_planes * space_count * cells_y * cells_z
    vmem = pl.BlockSpec(memory_space=pltpu.VMEM)
    dma = pltpu.SemaphoreType.DMA
    slab_rows = (RING, HALO, 16, 128)
    tile = (8, 128)
    sems = [5, 2] + [RING] * 4 + [2, 2] + [RING] * 12
    filtered, gram = pl.pallas_call(
        lambda *refs: step_kernel(1.0 / cells, *refs),
        out_shape=(
            jax.ShapeDtypeStruct(slab_rows, BF),
            jax.ShapeDtypeStruct(tile, F32),
        ),
        in_specs=[pl.BlockSpec(memory_space=pltpu.HBM)] * 6,
        out_specs=(vmem, vmem),
        scratch_shapes=[
            pltpu.SMEM(atom_planes.shape, jnp.int32),
            pltpu.VMEM(orbitals.shape, F32),
            pltpu.VMEM(orbitals.shape, F32),
            pltpu.VMEM(potential.shape, F32),
            pltpu.VMEM(strengths.shape[::-1], F32),
            pltpu.VMEM((HALO, cells_y, band_dev, cells_z), F32),
            pltpu.VMEM((2, ATOM_DEV, NPJ, BOX, 8, cells_z), BF),
            pltpu.VMEM((ATOM_DEV * ROWS, 128), BF),
            pltpu.VMEM((ATOM_DEV * ROWS, 128), BF),
            pltpu.VMEM(slab_rows, BF),
            pltpu.VMEM(slab_rows, BF),
            pltpu.VMEM((4, GROUP, HALO, 16, 128), BF),
            pltpu.VMEM(slab_rows, BF),
            pltpu.VMEM(slab_rows, BF),
            pltpu.VMEM((2, ATOM_DEV, PAD + 2 * BOX, 32, 128), BF),
            pltpu.VMEM((ATOM_DEV, PAD + 2 * BOX, 32, 128), BF),
            pltpu.VMEM((ATOM_DEV * ROWS, 128), BF),
            pltpu.VMEM((ATOM_DEV * ROWS, 128), BF),
            pltpu.VMEM((ATOM_DEV, 192, 128), BF),
            pltpu.VMEM((GROUP, 12, 16, 128), F32),
            pltpu.VMEM((RING,) + tile, F32),
            pltpu.VMEM((GROUP,) + tile, F32),
            pltpu.VMEM((4, 16, 128), BF),
            pltpu.VMEM((8, 4, 16, 128), BF),
            pltpu.VMEM((RING,) + tile, F32),
            pltpu.VMEM((COLUMNS,) + tile, F32),
            pltpu.VMEM((COLUMNS,) + tile, F32),
            pltpu.VMEM(tile, F32),
            pltpu.VMEM((RING,) + tile, F32),
        ]
        + [dma((n,)) for n in sems],
        compiler_params=pltpu.CompilerParams(
            collective_id=0, has_side_effects=True, vmem_limit_bytes=50 << 20
        ),
        name="filter_step",
    )(
        *(
            pltpu.with_memory_space_constraint(operand, pltpu.HBM)
            for operand in (
                atom_planes, orbitals, previous, potential, projectors, strengths.T
            )
        )
    )
    filtered = filtered.reshape(RING, HALO, 2, band_dev, cells_z)
    filtered = filtered.transpose(3, 1, 0, 2, 4).reshape(orbitals.shape)
    return filtered, gram[:2, :8], gram[:2, 8:16]


def solution(mesh):
    in_specs = (
        P("band", "space", None, None),
        P("band", "space", None, None),
        P("space", None, None),
        P("space", None, None, None, None),
        P(),
        P(),
    )
    out_specs = (P("band", "space", None, None), P("space", "band"), P("space", "band"))
    return jax.shard_map(
        shards, mesh=mesh, in_specs=in_specs, out_specs=out_specs, check_vma=False
    )
```

```python
import jax
import jax.numpy as jnp
from jax import lax
from jax.experimental import pallas as pl
from jax.experimental.pallas import tpu as pltpu
from jax.sharding import PartitionSpec as P

MESH = pl.DeviceIdType.MESH
BF = jnp.bfloat16
F32 = jnp.float32

HALO = 6
BOX = 6
NPJ = 9
ATOM_DEV = 4
RING = 16
GROUP = 8
COLUMNS = 16
SLABS = 32
PAD = BOX - 1
ROWS = 2 * BOX * NPJ
WINDOWS = (0, 96, 208, 304)
CHIP_ORDER = (4, 3, 5, 2, 6, 1, 7)
ORDER = (8, 9, 7, 6, 10, 5, 11, 4, 12, 3, 13, 2, 14, 1, 15)

stencil_weights = (
    -5369.0 / 1800.0,
    12.0 / 7.0,
    -15.0 / 56.0,
    10.0 / 189.0,
    -1.0 / 112.0,
    2.0 / 1925.0,
    -1.0 / 16632.0,
)
center = 5.5
halfwidth = 5.5
gain = 2.0 / halfwidth


def nt_dot(a, b):
    return lax.dot_general(a, b, (((1,), (1,)), ((), ())), preferred_element_type=F32)


def step_kernel(
    scale,
    planes_in,
    psi_in,
    prev_in,
    pot_in,
    proj_ref,
    strength_in,
    filtered_ref,
    gram_ref,
    planes_ref,
    psi_ref,
    prev_ref,
    pot_ref,
    strength_ref,
    psi_rows,
    near,
    own_rows,
    far_rows,
    psi_send,
    local_send,
    window,
    local_got,
    filt_send,
    proj,
    proj_low,
    far_got,
    low_got,
    spread,
    along_x,
    coef_send,
    coef_pair,
    coef_part,
    coef_got,
    coef_all,
    gram_xy_send,
    gram_xy_got,
    gram_z_send,
    gram_z_got,
    load_sem,
    near_sem,
    psi_ss,
    psi_rs,
    halo_ss,
    halo_rs,
    proj_ss,
    proj_rs,
    local_ss,
    local_rs,
    red_ss,
    red_rs,
    all_ss,
    all_rs,
    filt_ss,
    filt_rs,
    gxy_ss,
    gxy_rs,
    gz_ss,
    gz_rs,
):
    space = lax.axis_index("space")
    band = lax.axis_index("band")
    column, half = space // 2, lax.rem(space, 2)
    me = half * GROUP + band

    def ring(k):
        return lax.rem(me + k, RING)

    def at_ring(index):
        return {"space": column * 2 + index // GROUP, "band": lax.rem(index, GROUP)}

    def at_column(col):
        return {"space": lax.rem(col + COLUMNS, COLUMNS) * 2 + half, "band": band}

    def remote(src, dst, ssem, rsem, device):
        return pltpu.make_async_remote_copy(
            src_ref=src, dst_ref=dst, send_sem=ssem, recv_sem=rsem,
            device_id=device, device_id_type=MESH,
        )

    mirror = (1 - half) * GROUP + (3 - band // 2) * 2 + lax.rem(band, 2)

    barrier = pltpu.get_barrier_semaphore()
    peers = [at_ring(ring(k)) for k in ORDER]
    peers += [at_column(column + k) for k in ORDER]
    for peer in peers:
        pl.semaphore_signal(barrier, inc=1, device_id=peer, device_id_type=MESH)

    loads = [
        pltpu.make_async_copy(source, target, load_sem.at[i])
        for i, (source, target) in enumerate(
            (
                (psi_in, psi_ref),
                (strength_in, strength_ref),
                (planes_in, planes_ref),
                (pot_in, pot_ref),
                (prev_in, prev_ref),
            )
        )
    ]
    fetches = {}
    for i, pair in ((1, mirror), (0, me)):
        block = pl.ds(pl.multiple_of(pair // 4 * 8, 8), 8)
        fetch = pltpu.make_async_copy(proj_ref.at[:, :, :, block, :], near.at[i], near_sem.at[i])
        fetch.start()
        fetches[i] = fetch
        if i:
            loads[0].start()
    for load in loads[1:]:
        load.start()

    pick_row = lax.broadcasted_iota(jnp.int32, (32, 128), 0)
    pick_from = lax.broadcasted_iota(jnp.int32, (32, 128), 1)

    def pick_rows(i, pair, rows_ref):
        wanted = 8 * (pick_row >> 1) + 2 * lax.rem(pair, 4) + (pick_row & 1)
        pick = jnp.where(pick_from == wanted, 1.0, 0.0).astype(BF)
        fetches[i].wait()
        flat = near[i].reshape(ATOM_DEV * ROWS * 4, 128)
        for g in range(14):
            first = min(128 * g, ATOM_DEV * ROWS * 4 - 128)
            rows = jnp.dot(pick, flat[first : first + 128], preferred_element_type=F32)
            rows_ref[first // 4 : first // 4 + 32] = rows.astype(BF)

    pick_rows(1, mirror, far_rows)

    loads[0].wait()

    def pack(p, carry):
        turned = jnp.swapaxes(psi_ref[:, p], 0, 1)
        psi_rows[p] = turned
        psi_send[:, p] = turned.reshape(RING, 16, 128).astype(BF)
        return carry

    lax.fori_loop(0, HALO, pack, 0)
    window[1 + half, band] = psi_send[me]

    pl.semaphore_wait(barrier, len(peers))

    sends = []
    far_copy = remote(far_rows, far_got, proj_ss.at[0], proj_rs.at[0], at_ring(mirror))

    def low_copy(rows_ref, col):
        return remote(rows_ref, low_got, proj_ss.at[1], proj_rs.at[1], at_column(col))

    far_copy.start()
    sends.append(far_copy)
    pick_rows(0, me, own_rows)

    @pl.when(half == 1)
    def _():
        low_copy(own_rows, column + 1).start()

    for k in ORDER:
        copy = remote(
            psi_send.at[ring(k)], window.at[1 + half, band], psi_ss.at[k], psi_rs.at[k],
            at_ring(ring(k)),
        )
        copy.start()
        sends.append(copy)

    for k in range(3):
        table = proj.at[k - 1] if k else proj_low
        table[:, 0:PAD] = jnp.zeros((ATOM_DEV, PAD, 32, 128), BF)
        table[:, PAD + BOX :] = jnp.zeros((ATOM_DEV, BOX, 32, 128), BF)

    row = lax.broadcasted_iota(jnp.int32, (192, 128), 0)
    source_row = lax.broadcasted_iota(jnp.int32, (192, 128), 1) - 12 * (row & 15) - (row >> 4)
    for a in range(ATOM_DEV):
        hit = (source_row == ROWS * a - WINDOWS[a]) & ((row & 15) < NPJ)
        spread[a] = jnp.where(hit, 1.0, 0.0).astype(BF)

    def expand(rows_ref, table):
        for a in range(ATOM_DEV):
            rows = rows_ref[WINDOWS[a] : WINDOWS[a] + 128]
            moved = jnp.dot(spread[a], rows, preferred_element_type=F32)
            table[a, PAD : PAD + BOX] = moved.astype(BF).reshape(BOX, 32, 128)

    expand(own_rows, proj.at[half])

    loads[1].wait()
    loads[2].wait()
    lane_row = lax.broadcasted_iota(jnp.int32, (128, 128), 0)
    lane_col = lax.broadcasted_iota(jnp.int32, (128, 128), 1)
    own_lane = lax.broadcasted_iota(jnp.int32, (NPJ, 128), 0)
    own_lane = own_lane == (lax.broadcasted_iota(jnp.int32, (NPJ, 128), 1) & 15)
    slabs = [lax.rem(2 * column - 1 + k + SLABS, SLABS) for k in range(3)]
    levels = []
    for k in range(3):
        take = jnp.where(lane_row == slabs[k] * ATOM_DEV + (lane_col >> 5), 1.0, 0.0)
        spread_levels = jnp.dot(
            strength_ref[...], take, precision=lax.Precision.HIGHEST, preferred_element_type=F32
        )
        picked = jnp.where(own_lane, spread_levels, 0.0)
        levels.append(gain * jnp.sum(picked, axis=0, keepdims=True))

    loads[3].wait()
    loads[4].wait()
    def local_terms(p, carry):
        field = psi_rows[p]
        flat = field.reshape(256, 128)
        total = (3.0 * stencil_weights[0]) * field
        for m in range(1, HALO + 1):
            ahead = jnp.concatenate([field[m:], field[:m]], axis=0)
            behind = jnp.concatenate([field[32 - m :], field[: 32 - m]], axis=0)
            turned = pltpu.roll(flat, m, 1) + pltpu.roll(flat, 128 - m, 1)
            total = total + stencil_weights[m] * (ahead + behind + turned.reshape(32, 8, 128))
        level = pot_ref[p][:, None, :] - center
        local = gain * (level * field - 0.5 * total) - jnp.swapaxes(prev_ref[:, p], 0, 1)
        local_send[:, p] = local.reshape(RING, 16, 128).astype(BF)
        return carry

    lax.fori_loop(0, HALO, local_terms, 0)
    local_got[me] = local_send[me]

    for k in (1, 15, 2, 14, 3, 13, 4, 12, 5, 11, 6, 10, 7, 9, 8):
        copy = remote(
            local_send.at[ring(k)], local_got.at[me], local_ss.at[k], local_rs.at[k],
            at_ring(ring(k)),
        )
        copy.start()
        sends.append(copy)

    far_copy.wait_recv()

    @pl.when(half == 0)
    def _():
        low_copy(far_got, column + 1).start()

    for k in (0,) + ORDER:
        source = lax.rem(me - k + RING, RING)
        side, group = source // GROUP, lax.rem(source, GROUP)
        piece = window.at[1 + side, group]
        if k:
            remote(piece, piece, psi_ss.at[k], psi_rs.at[k], at_ring(source)).wait_recv()
        copy = remote(
            piece, window.at[3 - 3 * side, group], halo_ss.at[k], halo_rs.at[k],
            at_column(column + 2 * side - 1),
        )
        copy.start()
        sends.append(copy)

    def start(k, a):
        return jnp.clip(planes_ref[slabs[k] * ATOM_DEV + a] - slabs[k] * HALO, 0, HALO - 1)

    starts = [[start(k, a) for a in range(ATOM_DEV)] for k in range(3)]

    def stack(k, plane):
        table = proj.at[k - 1] if k else proj_low
        rows = [table[a, plane - starts[k][a] + PAD] for a in range(ATOM_DEV)]
        return jnp.concatenate(rows, axis=0)

    def psi_plane(m, p):
        return window[m, :, p].reshape(128, 128)

    def psi_lanes(m):
        return jnp.concatenate([psi_plane(m, p) for p in range(HALO)], axis=1)

    def stack_lanes(k, first):
        return jnp.concatenate([stack(k, first + p) for p in range(HALO)], axis=1)

    expand(far_got, proj.at[1 - half])
    coef_mid = nt_dot(psi_lanes(1), stack_lanes(1, 0)) + nt_dot(psi_lanes(2), stack_lanes(1, HALO))
    coef_high = nt_dot(psi_lanes(2), stack_lanes(2, 0))
    low_copy(far_got, column - 1).wait_recv()
    expand(low_got, proj_low)
    coef_low = nt_dot(psi_lanes(1), stack_lanes(0, HALO))
    for k in (0,) + ORDER:
        source = lax.rem(me - k + RING, RING)
        side, group = source // GROUP, lax.rem(source, GROUP)
        slot = window.at[3 - 3 * side, group]
        remote(
            slot, slot, halo_ss.at[k], halo_rs.at[k], at_column(column + 2 * side - 1)
        ).wait_recv()
    coef_low = coef_low + nt_dot(psi_lanes(0), stack_lanes(0, 0))
    coef_high = coef_high + nt_dot(psi_lanes(3), stack_lanes(2, HALO))

    lane = lax.broadcasted_iota(jnp.int32, (GROUP, 8, 128), 2)
    even_row = (lane & 16) == 0

    def swap(value):
        up = pltpu.roll(value, 16, 2)
        down = pltpu.roll(value, 112, 2)
        return jnp.where(even_row, down, up)

    folded = []
    for coef in (coef_low, coef_mid, coef_high):
        parts = coef.reshape(GROUP, 2, 8, 128)
        mixed = jnp.where(even_row, parts[:, 0], parts[:, 1])
        folded.append(mixed + swap(mixed))
    coef_send[0:GROUP] = jnp.where(even_row, folded[0], folded[1])
    coef_send[GROUP:] = folded[2]

    core = lax.rem(band, 2)
    chip = me // 2
    sibling = {"band": band + 1 - 2 * core}
    kept, given = pl.ds(core * GROUP, GROUP), pl.ds((1 - core) * GROUP, GROUP)
    copy = remote(coef_send.at[given], coef_pair, red_ss.at[0], red_rs.at[0], sibling)
    copy.start()
    sends.append(copy)
    copy.wait_recv()
    coef_part[...] = (coef_send[kept] + coef_pair[...]).reshape(4, 16, 128).astype(BF)
    coef_got[chip] = coef_part[...]
    for k in CHIP_ORDER:
        copy = remote(
            coef_part, coef_got.at[chip], all_ss.at[k], all_rs.at[k], at_ring(ring(2 * k))
        )
        copy.start()
        sends.append(copy)

    def stencil_x(group, carry):
        planes = window[:, group].reshape(24, 16, 128).astype(F32)
        total = jnp.zeros((12, 16, 128), F32)
        for m in range(1, HALO + 1):
            pair = planes[HALO - m : 18 - m] + planes[HALO + m : 18 + m]
            total = total + (-0.5 * gain * stencil_weights[m]) * pair
        along_x[group] = total
        return carry

    lax.fori_loop(0, GROUP, stencil_x, 0)

    for k in CHIP_ORDER:
        slot = coef_got.at[lax.rem(chip - k + 8, 8)]
        remote(slot, slot, all_ss.at[k], all_rs.at[k], at_ring(ring(2 * k))).wait_recv()
    coef_all[kept] = jnp.sum(coef_got[...].astype(F32), axis=0).reshape(GROUP, 8, 128)
    copy = remote(coef_all.at[kept], coef_all.at[kept], red_ss.at[1], red_rs.at[1], sibling)
    copy.start()
    sends.append(copy)
    remote(coef_all.at[given], coef_all.at[given], red_ss.at[1], red_rs.at[1], sibling).wait_recv()

    shared = coef_all[0:GROUP]
    crossed = swap(shared)
    full = [
        jnp.where(even_row, shared, crossed),
        jnp.where(even_row, crossed, shared),
        coef_all[GROUP:],
    ]
    weights = []
    for k in range(3):
        weighted = full[k] * levels[k]
        rows = [jnp.where(even_row, weighted, 0.0), jnp.where(even_row, 0.0, weighted)]
        weights.append(jnp.stack(rows, axis=1).reshape(128, 128).astype(BF))

    for k in ORDER:
        slot = local_got.at[lax.rem(me - k + RING, RING)]
        remote(slot, slot, local_ss.at[k], local_rs.at[k], at_ring(ring(k))).wait_recv()

    gram = jnp.zeros((128, 256), F32)
    for m in (1, 2):
        side = m - 1
        both = jnp.concatenate([weights[m - 1], weights[m]], axis=1)
        rows = pl.ds(side * GROUP, GROUP)

        values = []
        for p in range(HALO):
            table = jnp.concatenate([stack(m - 1, HALO + p), stack(m, p)], axis=0)
            term = jnp.dot(both, table, preferred_element_type=F32)
            term = term + along_x[:, side * HALO + p].reshape(128, 128)
            term = term + local_got[rows, p].reshape(128, 128).astype(F32)
            values.append(term.astype(BF))
            filt_send[rows, p] = values[p].reshape(GROUP, 16, 128)
        for k in ORDER:
            target = ring(k)

            @pl.when(target // GROUP == side)
            def _():
                remote(
                    filt_send.at[target], filtered_ref.at[me], filt_ss.at[k], filt_rs.at[k],
                    at_ring(target),
                ).start()

        value = jnp.concatenate(values, axis=1)
        gram = gram + nt_dot(value, jnp.concatenate([value, psi_lanes(m)], axis=0))

    filtered_ref[me] = filt_send[me]

    even_eight = (lane & 8) == 0
    parts = gram.reshape(GROUP, 2, 8, 256)
    left = jnp.where(even_eight, parts[:, 0, :, :128], parts[:, 1, :, :128])
    right = jnp.where(even_eight, parts[:, 0, :, 128:], parts[:, 1, :, 128:])
    merged = jnp.where(
        even_eight, left + pltpu.roll(left, 120, 2), right + pltpu.roll(right, 8, 2)
    )
    merged = merged.reshape(64, 128)
    for c in range(COLUMNS):
        gram_xy_send[c] = merged[4 * c : 4 * c + 4]
    gram_xy_got[column] = gram_xy_send[column]
    for k in ORDER:
        to = lax.rem(column + k, COLUMNS)
        copy = remote(
            gram_xy_send.at[to], gram_xy_got.at[column], gxy_ss.at[k], gxy_rs.at[k], at_column(to)
        )
        copy.start()
        sends.append(copy)
    for k in ORDER:
        source = lax.rem(column - k + COLUMNS, COLUMNS)
        slot = gram_xy_got.at[source]
        remote(slot, slot, gxy_ss.at[k], gxy_rs.at[k], at_column(source)).wait_recv()
    rows_x = jnp.sum(gram_xy_got[...], axis=0)
    gram_z_send[...] = rows_x
    gram_z_got[me] = rows_x
    for k in ORDER:
        copy = remote(gram_z_send, gram_z_got.at[me], gz_ss.at[k], gz_rs.at[k], at_ring(ring(k)))
        copy.start()
        sends.append(copy)
    for k in ORDER:
        slot = gram_z_got.at[lax.rem(me - k + RING, RING)]
        remote(gram_z_send, slot, gz_ss.at[k], gz_rs.at[k], at_ring(ring(k))).wait_recv()
    total = jnp.sum(gram_z_got[...], axis=0) * scale
    total = jnp.concatenate([total, total], axis=0)
    total = pltpu.roll(total, lax.rem(128 - 16 * band, 128), 1)
    gram_ref[...] = jnp.where(half == 0, total, pltpu.roll(total, 6, 0))

    for k in ORDER:
        copy = remote(
            filt_send.at[ring(k)], filtered_ref.at[lax.rem(me - k + RING, RING)],
            filt_ss.at[k], filt_rs.at[k], at_ring(ring(k)),
        )
        copy.wait_recv()
        copy.wait_send()
    low_copy(far_got, column + 1).wait_send()
    for copy in sends:
        copy.wait_send()


def shards(orbitals, previous, potential, projectors, strengths, atom_planes):
    band_dev, slab_planes, cells_y, cells_z = orbitals.shape
    space_count, band_count = lax.axis_size("space"), lax.axis_size("band")
    cells = slab_planes * space_count * cells_y * cells_z
    vmem = pl.BlockSpec(memory_space=pltpu.VMEM)
    dma = pltpu.SemaphoreType.DMA
    slab_rows = (RING, HALO, 16, 128)
    tile = (8, 128)
    sems = [5, 2] + [RING] * 4 + [2, 2] + [RING] * 12
    filtered, gram = pl.pallas_call(
        lambda *refs: step_kernel(1.0 / cells, *refs),
        out_shape=(
            jax.ShapeDtypeStruct(slab_rows, BF),
            jax.ShapeDtypeStruct(tile, F32),
        ),
        in_specs=[pl.BlockSpec(memory_space=pltpu.HBM)] * 6,
        out_specs=(vmem, vmem),
        scratch_shapes=[
            pltpu.SMEM(atom_planes.shape, jnp.int32),
            pltpu.VMEM(orbitals.shape, F32),
            pltpu.VMEM(orbitals.shape, F32),
            pltpu.VMEM(potential.shape, F32),
            pltpu.VMEM(strengths.shape[::-1], F32),
            pltpu.VMEM((HALO, cells_y, band_dev, cells_z), F32),
            pltpu.VMEM((2, ATOM_DEV, NPJ, BOX, 8, cells_z), BF),
            pltpu.VMEM((ATOM_DEV * ROWS, 128), BF),
            pltpu.VMEM((ATOM_DEV * ROWS, 128), BF),
            pltpu.VMEM(slab_rows, BF),
            pltpu.VMEM(slab_rows, BF),
            pltpu.VMEM((4, GROUP, HALO, 16, 128), BF),
            pltpu.VMEM(slab_rows, BF),
            pltpu.VMEM(slab_rows, BF),
            pltpu.VMEM((2, ATOM_DEV, PAD + 2 * BOX, 32, 128), BF),
            pltpu.VMEM((ATOM_DEV, PAD + 2 * BOX, 32, 128), BF),
            pltpu.VMEM((ATOM_DEV * ROWS, 128), BF),
            pltpu.VMEM((ATOM_DEV * ROWS, 128), BF),
            pltpu.VMEM((ATOM_DEV, 192, 128), BF),
            pltpu.VMEM((GROUP, 12, 16, 128), F32),
            pltpu.VMEM((RING,) + tile, F32),
            pltpu.VMEM((GROUP,) + tile, F32),
            pltpu.VMEM((4, 16, 128), BF),
            pltpu.VMEM((8, 4, 16, 128), BF),
            pltpu.VMEM((RING,) + tile, F32),
            pltpu.VMEM((COLUMNS, 4, 128), F32),
            pltpu.VMEM((COLUMNS, 4, 128), F32),
            pltpu.VMEM((4, 128), F32),
            pltpu.VMEM((RING, 4, 128), F32),
        ]
        + [dma((n,)) for n in sems],
        compiler_params=pltpu.CompilerParams(
            collective_id=0, has_side_effects=True, vmem_limit_bytes=50 << 20
        ),
        name="filter_step",
    )(
        *(
            pltpu.with_memory_space_constraint(operand, pltpu.HBM)
            for operand in (
                atom_planes, orbitals, previous, potential, projectors, strengths.T
            )
        )
    )
    filtered = filtered.reshape(RING, HALO, 2, band_dev, cells_z)
    filtered = filtered.transpose(3, 1, 0, 2, 4).reshape(orbitals.shape)
    return filtered, gram[:2, :8], gram[:2, 8:16]


def solution(mesh):
    in_specs = (
        P("band", "space", None, None),
        P("band", "space", None, None),
        P("space", None, None),
        P("space", None, None, None, None),
        P(),
        P(),
    )
    out_specs = (P("band", "space", None, None), P("space", "band"), P("space", "band"))
    return jax.shard_map(
        shards, mesh=mesh, in_specs=in_specs, out_specs=out_specs, check_vma=False
    )
```

```python
import jax
import jax.numpy as jnp
from jax import lax
from jax.experimental import pallas as pl
from jax.experimental.pallas import tpu as pltpu
from jax.sharding import PartitionSpec as P

MESH = pl.DeviceIdType.MESH
BF = jnp.bfloat16
F32 = jnp.float32

HALO = 6
BOX = 6
NPJ = 9
ATOM_DEV = 4
RING = 16
GROUP = 8
COLUMNS = 16
SLABS = 32
PAD = BOX - 1
ROWS = 2 * BOX * NPJ
WINDOWS = (0, 96, 208, 304)
CHIP_ORDER = (4, 3, 5, 2, 6, 1, 7)
ORDER = (8, 9, 7, 6, 10, 5, 11, 4, 12, 3, 13, 2, 14, 1, 15)

stencil_weights = (
    -5369.0 / 1800.0,
    12.0 / 7.0,
    -15.0 / 56.0,
    10.0 / 189.0,
    -1.0 / 112.0,
    2.0 / 1925.0,
    -1.0 / 16632.0,
)
center = 5.5
halfwidth = 5.5
gain = 2.0 / halfwidth


def nt_dot(a, b):
    return lax.dot_general(a, b, (((1,), (1,)), ((), ())), preferred_element_type=F32)


def step_kernel(
    scale,
    planes_in,
    psi_in,
    prev_in,
    pot_in,
    proj_ref,
    strength_in,
    filtered_ref,
    gram_ref,
    planes_ref,
    psi_ref,
    prev_ref,
    pot_ref,
    strength_ref,
    psi_rows,
    near,
    own_rows,
    far_rows,
    psi_send,
    local_send,
    window,
    local_got,
    filt_send,
    proj,
    proj_low,
    far_got,
    low_got,
    spread,
    along_x,
    coef_send,
    coef_pair,
    coef_part,
    coef_got,
    coef_all,
    gram_xy_send,
    gram_xy_got,
    gram_z_send,
    gram_z_got,
    load_sem,
    near_sem,
    psi_ss,
    psi_rs,
    halo_ss,
    halo_rs,
    proj_ss,
    proj_rs,
    local_ss,
    local_rs,
    red_ss,
    red_rs,
    all_ss,
    all_rs,
    filt_ss,
    filt_rs,
    gxy_ss,
    gxy_rs,
    gz_ss,
    gz_rs,
):
    space = lax.axis_index("space")
    band = lax.axis_index("band")
    column, half = space // 2, lax.rem(space, 2)
    me = half * GROUP + band

    def ring(k):
        return lax.rem(me + k, RING)

    def at_ring(index):
        return {"space": column * 2 + index // GROUP, "band": lax.rem(index, GROUP)}

    def at_column(col):
        return {"space": lax.rem(col + COLUMNS, COLUMNS) * 2 + half, "band": band}

    def remote(src, dst, ssem, rsem, device):
        return pltpu.make_async_remote_copy(
            src_ref=src, dst_ref=dst, send_sem=ssem, recv_sem=rsem,
            device_id=device, device_id_type=MESH,
        )

    mirror = (1 - half) * GROUP + (3 - band // 2) * 2 + lax.rem(band, 2)

    barrier = pltpu.get_barrier_semaphore()
    peers = [at_ring(ring(k)) for k in ORDER]
    peers += [at_column(column + k) for k in ORDER]
    for peer in peers:
        pl.semaphore_signal(barrier, inc=1, device_id=peer, device_id_type=MESH)

    loads = [
        pltpu.make_async_copy(source, target, load_sem.at[i])
        for i, (source, target) in enumerate(
            (
                (psi_in, psi_ref),
                (strength_in, strength_ref),
                (planes_in, planes_ref),
                (pot_in, pot_ref),
                (prev_in, prev_ref),
            )
        )
    ]
    fetches = {}
    for i, pair in ((1, mirror), (0, me)):
        block = pl.ds(pl.multiple_of(pair // 4 * 8, 8), 8)
        fetch = pltpu.make_async_copy(proj_ref.at[:, :, :, block, :], near.at[i], near_sem.at[i])
        fetch.start()
        fetches[i] = fetch
        if i:
            loads[0].start()
    for load in loads[1:]:
        load.start()

    pick_row = lax.broadcasted_iota(jnp.int32, (32, 128), 0)
    pick_from = lax.broadcasted_iota(jnp.int32, (32, 128), 1)

    def pick_rows(i, pair, rows_ref):
        wanted = 8 * (pick_row >> 1) + 2 * lax.rem(pair, 4) + (pick_row & 1)
        pick = jnp.where(pick_from == wanted, 1.0, 0.0).astype(BF)
        fetches[i].wait()
        flat = near[i].reshape(ATOM_DEV * ROWS * 4, 128)
        for g in range(14):
            first = min(128 * g, ATOM_DEV * ROWS * 4 - 128)
            rows = jnp.dot(pick, flat[first : first + 128], preferred_element_type=F32)
            rows_ref[first // 4 : first // 4 + 32] = rows.astype(BF)

    pick_rows(1, mirror, far_rows)

    loads[0].wait()

    def pack(p, carry):
        turned = jnp.swapaxes(psi_ref[:, p], 0, 1)
        psi_rows[p] = turned
        psi_send[:, p] = turned.reshape(RING, 16, 128).astype(BF)
        return carry

    lax.fori_loop(0, HALO, pack, 0)
    window[1 + half, band] = psi_send[me]

    pl.semaphore_wait(barrier, len(peers))

    sends = []
    far_copy = remote(far_rows, far_got, proj_ss.at[0], proj_rs.at[0], at_ring(mirror))

    def low_copy(rows_ref, col):
        return remote(rows_ref, low_got, proj_ss.at[1], proj_rs.at[1], at_column(col))

    far_copy.start()
    sends.append(far_copy)
    pick_rows(0, me, own_rows)

    @pl.when(half == 1)
    def _():
        low_copy(own_rows, column + 1).start()

    for k in ORDER:
        copy = remote(
            psi_send.at[ring(k)], window.at[1 + half, band], psi_ss.at[k], psi_rs.at[k],
            at_ring(ring(k)),
        )
        copy.start()
        sends.append(copy)

    for k in range(3):
        table = proj.at[k - 1] if k else proj_low
        table[:, 0:PAD] = jnp.zeros((ATOM_DEV, PAD, 32, 128), BF)
        table[:, PAD + BOX :] = jnp.zeros((ATOM_DEV, BOX, 32, 128), BF)

    row = lax.broadcasted_iota(jnp.int32, (192, 128), 0)
    source_row = lax.broadcasted_iota(jnp.int32, (192, 128), 1) - 12 * (row & 15) - (row >> 4)
    for a in range(ATOM_DEV):
        hit = (source_row == ROWS * a - WINDOWS[a]) & ((row & 15) < NPJ)
        spread[a] = jnp.where(hit, 1.0, 0.0).astype(BF)

    def expand(rows_ref, table):
        for a in range(ATOM_DEV):
            rows = rows_ref[WINDOWS[a] : WINDOWS[a] + 128]
            moved = jnp.dot(spread[a], rows, preferred_element_type=F32)
            table[a, PAD : PAD + BOX] = moved.astype(BF).reshape(BOX, 32, 128)

    expand(own_rows, proj.at[half])

    loads[1].wait()
    loads[2].wait()
    lane_row = lax.broadcasted_iota(jnp.int32, (128, 128), 0)
    lane_col = lax.broadcasted_iota(jnp.int32, (128, 128), 1)
    own_lane = lax.broadcasted_iota(jnp.int32, (NPJ, 128), 0)
    own_lane = own_lane == (lax.broadcasted_iota(jnp.int32, (NPJ, 128), 1) & 15)
    slabs = [lax.rem(2 * column - 1 + k + SLABS, SLABS) for k in range(3)]
    levels = []
    for k in range(3):
        take = jnp.where(lane_row == slabs[k] * ATOM_DEV + (lane_col >> 5), 1.0, 0.0)
        spread_levels = jnp.dot(
            strength_ref[...], take, precision=lax.Precision.HIGHEST, preferred_element_type=F32
        )
        picked = jnp.where(own_lane, spread_levels, 0.0)
        levels.append(gain * jnp.sum(picked, axis=0, keepdims=True))

    loads[3].wait()
    loads[4].wait()
    def local_terms(p, carry):
        field = psi_rows[p]
        flat = field.reshape(256, 128)
        total = (3.0 * stencil_weights[0]) * field
        for m in range(1, HALO + 1):
            ahead = jnp.concatenate([field[m:], field[:m]], axis=0)
            behind = jnp.concatenate([field[32 - m :], field[: 32 - m]], axis=0)
            turned = pltpu.roll(flat, m, 1) + pltpu.roll(flat, 128 - m, 1)
            total = total + stencil_weights[m] * (ahead + behind + turned.reshape(32, 8, 128))
        level = pot_ref[p][:, None, :] - center
        local = gain * (level * field - 0.5 * total) - jnp.swapaxes(prev_ref[:, p], 0, 1)
        local_send[:, p] = local.reshape(RING, 16, 128).astype(BF)
        return carry

    lax.fori_loop(0, HALO, local_terms, 0)
    local_got[me] = local_send[me]

    for k in (1, 15, 2, 14, 3, 13, 4, 12, 5, 11):
        copy = remote(
            local_send.at[ring(k)], local_got.at[me], local_ss.at[k], local_rs.at[k],
            at_ring(ring(k)),
        )
        copy.start()
        sends.append(copy)

    far_copy.wait_recv()

    @pl.when(half == 0)
    def _():
        low_copy(far_got, column + 1).start()

    for k in (0,) + ORDER:
        source = lax.rem(me - k + RING, RING)
        side, group = source // GROUP, lax.rem(source, GROUP)
        piece = window.at[1 + side, group]
        if k:
            remote(piece, piece, psi_ss.at[k], psi_rs.at[k], at_ring(source)).wait_recv()
        copy = remote(
            piece, window.at[3 - 3 * side, group], halo_ss.at[k], halo_rs.at[k],
            at_column(column + 2 * side - 1),
        )
        copy.start()
        sends.append(copy)

    for k in (6, 10, 7, 9, 8):
        copy = remote(
            local_send.at[ring(k)], local_got.at[me], local_ss.at[k], local_rs.at[k],
            at_ring(ring(k)),
        )
        copy.start()
        sends.append(copy)

    def start(k, a):
        return jnp.clip(planes_ref[slabs[k] * ATOM_DEV + a] - slabs[k] * HALO, 0, HALO - 1)

    starts = [[start(k, a) for a in range(ATOM_DEV)] for k in range(3)]

    def stack(k, plane):
        table = proj.at[k - 1] if k else proj_low
        rows = [table[a, plane - starts[k][a] + PAD] for a in range(ATOM_DEV)]
        return jnp.concatenate(rows, axis=0)

    def psi_plane(m, p):
        return window[m, :, p].reshape(128, 128)

    def psi_lanes(m):
        return jnp.concatenate([psi_plane(m, p) for p in range(HALO)], axis=1)

    def stack_lanes(k, first):
        return jnp.concatenate([stack(k, first + p) for p in range(HALO)], axis=1)

    expand(far_got, proj.at[1 - half])
    coef_mid = nt_dot(psi_lanes(1), stack_lanes(1, 0)) + nt_dot(psi_lanes(2), stack_lanes(1, HALO))
    coef_high = nt_dot(psi_lanes(2), stack_lanes(2, 0))
    low_copy(far_got, column - 1).wait_recv()
    expand(low_got, proj_low)
    coef_low = nt_dot(psi_lanes(1), stack_lanes(0, HALO))
    for k in (0,) + ORDER:
        source = lax.rem(me - k + RING, RING)
        side, group = source // GROUP, lax.rem(source, GROUP)
        slot = window.at[3 - 3 * side, group]
        remote(
            slot, slot, halo_ss.at[k], halo_rs.at[k], at_column(column + 2 * side - 1)
        ).wait_recv()
    coef_low = coef_low + nt_dot(psi_lanes(0), stack_lanes(0, 0))
    coef_high = coef_high + nt_dot(psi_lanes(3), stack_lanes(2, HALO))

    lane = lax.broadcasted_iota(jnp.int32, (GROUP, 8, 128), 2)
    even_row = (lane & 16) == 0

    def swap(value):
        up = pltpu.roll(value, 16, 2)
        down = pltpu.roll(value, 112, 2)
        return jnp.where(even_row, down, up)

    folded = []
    for coef in (coef_low, coef_mid, coef_high):
        parts = coef.reshape(GROUP, 2, 8, 128)
        mixed = jnp.where(even_row, parts[:, 0], parts[:, 1])
        folded.append(mixed + swap(mixed))
    coef_send[0:GROUP] = jnp.where(even_row, folded[0], folded[1])
    coef_send[GROUP:] = folded[2]

    core = lax.rem(band, 2)
    chip = me // 2
    sibling = {"band": band + 1 - 2 * core}
    kept, given = pl.ds(core * GROUP, GROUP), pl.ds((1 - core) * GROUP, GROUP)
    copy = remote(coef_send.at[given], coef_pair, red_ss.at[0], red_rs.at[0], sibling)
    copy.start()
    sends.append(copy)
    copy.wait_recv()
    coef_part[...] = (coef_send[kept] + coef_pair[...]).reshape(4, 16, 128).astype(BF)
    coef_got[chip] = coef_part[...]
    for k in CHIP_ORDER:
        copy = remote(
            coef_part, coef_got.at[chip], all_ss.at[k], all_rs.at[k], at_ring(ring(2 * k))
        )
        copy.start()
        sends.append(copy)

    def stencil_x(group, carry):
        planes = window[:, group].reshape(24, 16, 128).astype(F32)
        total = jnp.zeros((12, 16, 128), F32)
        for m in range(1, HALO + 1):
            pair = planes[HALO - m : 18 - m] + planes[HALO + m : 18 + m]
            total = total + (-0.5 * gain * stencil_weights[m]) * pair
        along_x[group] = total
        return carry

    lax.fori_loop(0, GROUP, stencil_x, 0)

    for k in CHIP_ORDER:
        slot = coef_got.at[lax.rem(chip - k + 8, 8)]
        remote(slot, slot, all_ss.at[k], all_rs.at[k], at_ring(ring(2 * k))).wait_recv()
    coef_all[kept] = jnp.sum(coef_got[...].astype(F32), axis=0).reshape(GROUP, 8, 128)
    copy = remote(coef_all.at[kept], coef_all.at[kept], red_ss.at[1], red_rs.at[1], sibling)
    copy.start()
    sends.append(copy)
    remote(coef_all.at[given], coef_all.at[given], red_ss.at[1], red_rs.at[1], sibling).wait_recv()

    shared = coef_all[0:GROUP]
    crossed = swap(shared)
    full = [
        jnp.where(even_row, shared, crossed),
        jnp.where(even_row, crossed, shared),
        coef_all[GROUP:],
    ]
    weights = []
    for k in range(3):
        weighted = full[k] * levels[k]
        rows = [jnp.where(even_row, weighted, 0.0), jnp.where(even_row, 0.0, weighted)]
        weights.append(jnp.stack(rows, axis=1).reshape(128, 128).astype(BF))

    for k in ORDER:
        slot = local_got.at[lax.rem(me - k + RING, RING)]
        remote(slot, slot, local_ss.at[k], local_rs.at[k], at_ring(ring(k))).wait_recv()

    gram = jnp.zeros((128, 256), F32)
    for m in (1, 2):
        side = m - 1
        both = jnp.concatenate([weights[m - 1], weights[m]], axis=1)
        rows = pl.ds(side * GROUP, GROUP)

        values = []
        for p in range(HALO):
            table = jnp.concatenate([stack(m - 1, HALO + p), stack(m, p)], axis=0)
            term = jnp.dot(both, table, preferred_element_type=F32)
            term = term + along_x[:, side * HALO + p].reshape(128, 128)
            term = term + local_got[rows, p].reshape(128, 128).astype(F32)
            values.append(term.astype(BF))
            filt_send[rows, p] = values[p].reshape(GROUP, 16, 128)
        for k in ORDER:
            target = ring(k)

            @pl.when(target // GROUP == side)
            def _():
                remote(
                    filt_send.at[target], filtered_ref.at[me], filt_ss.at[k], filt_rs.at[k],
                    at_ring(target),
                ).start()

        value = jnp.concatenate(values, axis=1)
        gram = gram + nt_dot(value, jnp.concatenate([value, psi_lanes(m)], axis=0))

    filtered_ref[me] = filt_send[me]

    even_eight = (lane & 8) == 0
    parts = gram.reshape(GROUP, 2, 8, 256)
    left = jnp.where(even_eight, parts[:, 0, :, :128], parts[:, 1, :, :128])
    right = jnp.where(even_eight, parts[:, 0, :, 128:], parts[:, 1, :, 128:])
    merged = jnp.where(
        even_eight, left + pltpu.roll(left, 120, 2), right + pltpu.roll(right, 8, 2)
    )
    merged = merged.reshape(64, 128)
    for c in range(COLUMNS):
        gram_xy_send[c] = merged[4 * c : 4 * c + 4]
    gram_xy_got[column] = gram_xy_send[column]
    for k in ORDER:
        to = lax.rem(column + k, COLUMNS)
        copy = remote(
            gram_xy_send.at[to], gram_xy_got.at[column], gxy_ss.at[k], gxy_rs.at[k], at_column(to)
        )
        copy.start()
        sends.append(copy)
    for k in ORDER:
        source = lax.rem(column - k + COLUMNS, COLUMNS)
        slot = gram_xy_got.at[source]
        remote(slot, slot, gxy_ss.at[k], gxy_rs.at[k], at_column(source)).wait_recv()
    rows_x = jnp.sum(gram_xy_got[...], axis=0)
    gram_z_send[...] = rows_x
    gram_z_got[me] = rows_x
    for k in ORDER:
        copy = remote(gram_z_send, gram_z_got.at[me], gz_ss.at[k], gz_rs.at[k], at_ring(ring(k)))
        copy.start()
        sends.append(copy)
    for k in ORDER:
        slot = gram_z_got.at[lax.rem(me - k + RING, RING)]
        remote(gram_z_send, slot, gz_ss.at[k], gz_rs.at[k], at_ring(ring(k))).wait_recv()
    total = jnp.sum(gram_z_got[...], axis=0) * scale
    total = jnp.concatenate([total, total], axis=0)
    total = pltpu.roll(total, lax.rem(128 - 16 * band, 128), 1)
    gram_ref[...] = jnp.where(half == 0, total, pltpu.roll(total, 6, 0))

    for k in ORDER:
        copy = remote(
            filt_send.at[ring(k)], filtered_ref.at[lax.rem(me - k + RING, RING)],
            filt_ss.at[k], filt_rs.at[k], at_ring(ring(k)),
        )
        copy.wait_recv()
        copy.wait_send()
    low_copy(far_got, column + 1).wait_send()
    for copy in sends:
        copy.wait_send()


def shards(orbitals, previous, potential, projectors, strengths, atom_planes):
    band_dev, slab_planes, cells_y, cells_z = orbitals.shape
    space_count, band_count = lax.axis_size("space"), lax.axis_size("band")
    cells = slab_planes * space_count * cells_y * cells_z
    vmem = pl.BlockSpec(memory_space=pltpu.VMEM)
    dma = pltpu.SemaphoreType.DMA
    slab_rows = (RING, HALO, 16, 128)
    tile = (8, 128)
    sems = [5, 2] + [RING] * 4 + [2, 2] + [RING] * 12
    filtered, gram = pl.pallas_call(
        lambda *refs: step_kernel(1.0 / cells, *refs),
        out_shape=(
            jax.ShapeDtypeStruct(slab_rows, BF),
            jax.ShapeDtypeStruct(tile, F32),
        ),
        in_specs=[pl.BlockSpec(memory_space=pltpu.HBM)] * 6,
        out_specs=(vmem, vmem),
        scratch_shapes=[
            pltpu.SMEM(atom_planes.shape, jnp.int32),
            pltpu.VMEM(orbitals.shape, F32),
            pltpu.VMEM(orbitals.shape, F32),
            pltpu.VMEM(potential.shape, F32),
            pltpu.VMEM(strengths.shape[::-1], F32),
            pltpu.VMEM((HALO, cells_y, band_dev, cells_z), F32),
            pltpu.VMEM((2, ATOM_DEV, NPJ, BOX, 8, cells_z), BF),
            pltpu.VMEM((ATOM_DEV * ROWS, 128), BF),
            pltpu.VMEM((ATOM_DEV * ROWS, 128), BF),
            pltpu.VMEM(slab_rows, BF),
            pltpu.VMEM(slab_rows, BF),
            pltpu.VMEM((4, GROUP, HALO, 16, 128), BF),
            pltpu.VMEM(slab_rows, BF),
            pltpu.VMEM(slab_rows, BF),
            pltpu.VMEM((2, ATOM_DEV, PAD + 2 * BOX, 32, 128), BF),
            pltpu.VMEM((ATOM_DEV, PAD + 2 * BOX, 32, 128), BF),
            pltpu.VMEM((ATOM_DEV * ROWS, 128), BF),
            pltpu.VMEM((ATOM_DEV * ROWS, 128), BF),
            pltpu.VMEM((ATOM_DEV, 192, 128), BF),
            pltpu.VMEM((GROUP, 12, 16, 128), F32),
            pltpu.VMEM((RING,) + tile, F32),
            pltpu.VMEM((GROUP,) + tile, F32),
            pltpu.VMEM((4, 16, 128), BF),
            pltpu.VMEM((8, 4, 16, 128), BF),
            pltpu.VMEM((RING,) + tile, F32),
            pltpu.VMEM((COLUMNS, 4, 128), F32),
            pltpu.VMEM((COLUMNS, 4, 128), F32),
            pltpu.VMEM((4, 128), F32),
            pltpu.VMEM((RING, 4, 128), F32),
        ]
        + [dma((n,)) for n in sems],
        compiler_params=pltpu.CompilerParams(
            collective_id=0, has_side_effects=True, vmem_limit_bytes=50 << 20
        ),
        name="filter_step",
    )(
        *(
            pltpu.with_memory_space_constraint(operand, pltpu.HBM)
            for operand in (
                atom_planes, orbitals, previous, potential, projectors, strengths.T
            )
        )
    )
    filtered = filtered.reshape(RING, HALO, 2, band_dev, cells_z)
    filtered = filtered.transpose(3, 1, 0, 2, 4).reshape(orbitals.shape)
    return filtered, gram[:2, :8], gram[:2, 8:16]


def solution(mesh):
    in_specs = (
        P("band", "space", None, None),
        P("band", "space", None, None),
        P("space", None, None),
        P("space", None, None, None, None),
        P(),
        P(),
    )
    out_specs = (P("band", "space", None, None), P("space", "band"), P("space", "band"))
    return jax.shard_map(
        shards, mesh=mesh, in_specs=in_specs, out_specs=out_specs, check_vma=False
    )
```
